512 devices in a mesh: patch: 128 (over y, z, core), visit: 4 (over x).
Axes of the slice: x: 4, y: 8, z: 8, core: 2. Of those that a mesh axis runs over, the one named last changes fastest.
Arguments:
- pieces: bfloat16 [49152, 32, 128], P(('patch', 'visit')), may hold values from -16 to 16
- dest: int32 [49152, 1], P(('patch', 'visit')), may hold values from 0 to 127; in each aligned block of 96 rows (0 to 95, 96 to 191, ...) at most 2 rows name the same one
- offsets: int32 [49152], P(('patch', 'visit')), may hold values from 0 to 224
- kernel_index: int32 [49152], P(('patch', 'visit')), may hold values from 0 to 39
- weights: bfloat16 [49152], P(('patch', 'visit')), may hold values from 0.25 to 4
- basis_col: bfloat16 [14, 41], replicated, may hold values from -1 to 1
- basis_row: bfloat16 [14, 41], replicated, may hold values from -1 to 1
- coef_table: float32 [40, 14], replicated, may hold values from -2.4 to 2.4
- det_taps: bfloat16 [2, 21], replicated, may hold values from -1.25 to 1.25
Outputs:
- coadd: float32 [32768, 128], P(('patch', 'visit'))
- detection: float32 [32768, 128], P(('patch', 'visit'))
The draws below stay inside these ranges and needn't reach their ends.
Inputs may be any that keep to these rules, and one draw needn't show every extreme that they name: `dest`: at most 2 of the pieces of one device intersect one patch.
All inputs are finite; a program needn't handle non-finite values.
Results may differ from the reference program's by a relative error of at most 0.0062.
Values may be sent and summed in bfloat16 or wider, within the bound.
A program may use at most 64 MiB of HBM per device.

```python
import math
import jax
import jax.numpy as jnp
import numpy as np
from jax import lax

PIECES_DEV = 96
PR = 32
PW = 128
PH = 256
TAPS = 41
NB = 14
NK = 40
TD = 21
CAP = 2
PIECES = 49152
N_PATCH = 128


def touch_ends(result, stream_key, low, high):
    longest = result.shape.index(max(result.shape))
    spots = []
    for shift in (0, 1):
        where = [jax.random.randint(jax.random.fold_in(stream_key, axis), (), 0, length) for axis, length in enumerate(result.shape)]
        where[longest] = (where[longest] + shift) % result.shape[longest]
        spots.append(tuple(where))
    return result.at[spots[0]].set(low).at[spots[1]].set(high)


def levels(own_key, shape, shards, smallest, largest):
    def one(axis_at, parts):
        draws = jax.random.uniform(jax.random.fold_in(jax.random.fold_in(own_key, 6), axis_at), (parts,), jnp.float32, smallest / len(shards), largest / len(shards))
        return jnp.repeat(jnp.exp(draws), shape[axis_at] // parts).reshape((-1,) + (1,) * (len(shape) - axis_at - 1))

    loudness = one(*shards[0])
    for cut in shards[1:]:
        loudness = loudness * one(*cut)
    return loudness


def deal_out(key, own, number, rows, amount, top, bound, slope):
    sequence = jax.random.permutation(key, amount)
    crowded, ordinary = portions_of(amount, rows * top, bound, slope, True), portions_of(amount, rows * top, bound, slope, False)
    places = jnp.arange(amount)

    def named(lengths, offset_by):
        used = int((lengths > 0).sum())
        fixed = max(1, used // 4)
        moved = fixed + (places - fixed + offset_by * (used - fixed)) % max(1, amount - fixed)
        return jnp.zeros((amount,), jnp.int32).at[sequence[jnp.where(places < fixed, places, moved)]].set(jnp.asarray(lengths, jnp.int32))

    lengths = jnp.where(number % 4 == 0, named(crowded, number // 4), named(ordinary, number - number // 4 - 1))
    mixed = jax.random.permutation(jax.random.fold_in(own, 3), amount)
    donor, sink = mixed[0:amount // 2 * 2:2], mixed[1:amount // 2 * 2:2]
    room = jnp.minimum(lengths[donor] - 1, bound - lengths[sink]) // 2
    room = jnp.where((donor == sequence[0]) | (sink == sequence[0]) | (lengths[sink] == 0), 0, jnp.maximum(room, 0))
    moved = jax.random.randint(jax.random.fold_in(own, 4), (amount // 2,), 0, 1 << 20) % (room + 1)
    lengths = lengths.at[donor].add(-moved).at[sink].add(moved)
    members = jnp.searchsorted(jnp.cumsum(lengths), jnp.arange(rows * top), side="right").astype(jnp.int32)
    grid = members.reshape(top, rows).T
    grid = grid[jax.random.permutation(jax.random.fold_in(own, 1), rows)]
    offset_by = jax.random.randint(jax.random.fold_in(own, 2), (rows, 1), 0, top)
    return jnp.take_along_axis(grid, (jnp.arange(top)[None, :] + offset_by) % top, axis=1)


def portions_of(amount, total, most, slope, full):
    loads = [(1 << 20) // math.isqrt(rank ** slope) + 1 for rank in range(1, amount + 1)]
    largest = most if full else min(most, max(-(-total // amount), total * loads[0] // sum(loads)))
    least = 1 if total - largest >= amount - 1 else 0
    counts, rest = [largest] + [least] * (amount - 1), total - largest - least * (amount - 1)
    while rest > 0:
        free = [i for i in range(1, amount) if counts[i] < largest] or [i for i in range(1, amount) if counts[i] < most]
        mass, budget = sum([loads[i] for i in free]), rest
        for i in free:
            extra = min(most - counts[i], max(1, budget * loads[i] // mass), rest)
            counts[i] = counts[i] + extra
            rest = rest - extra
    return np.array(counts)


def normal_values(stream_key, extent, deviation, most, cuts=(), held_as=jnp.bfloat16):
    loudness = levels(stream_key, extent, cuts, -0.22, 0.18) if cuts else 1.0
    array = jax.random.normal(stream_key, extent, jnp.float32) * deviation * loudness
    return jnp.minimum(jnp.maximum(array, -most), most).astype(held_as)


def setup_inputs(seed: int = 0) -> dict:
    key_list = jax.random.split(jax.random.key(seed), 10)
    pieces = normal_values(key_list[0], (PIECES, PR, PW), 3.0, 16.0, ((0, 512),))
    dest_keys = jax.random.split(jax.random.fold_in(key_list[1], 1), PIECES // PIECES_DEV)
    dest_turns = jax.random.permutation(jax.random.fold_in(key_list[1], 3), PIECES // PIECES_DEV)
    dest = jax.vmap(lambda own, number: deal_out(jax.random.fold_in(key_list[1], 2), own, number, PIECES_DEV, N_PATCH, 1, CAP, 2))(dest_keys, dest_turns).reshape((PIECES, 1))
    offsets = touch_ends(jax.random.randint(key_list[2], (PIECES,), 0, PH - PR + 1), jax.random.fold_in(key_list[2], 1), 0, PH - PR).astype(jnp.int32)
    kernel_index = touch_ends(jax.random.randint(key_list[3], (PIECES,), 0, NK), jax.random.fold_in(key_list[3], 1), 0, NK - 1).astype(jnp.int32)
    weights = jnp.clip(jnp.exp(math.log(4.0) - 2.7725887 * jax.random.uniform(key_list[4], (PIECES,), jnp.float32) ** levels(key_list[4], (PIECES,), ((0, 512),), -0.2, 0.2)), 0.25, 4.0).astype(jnp.bfloat16)
    basis_col = normal_values(key_list[5], (NB, TAPS), TAPS ** -0.5, 1.0)
    basis_row = normal_values(key_list[6], (NB, TAPS), TAPS ** -0.5, 1.0)
    coef_table = normal_values(key_list[7], (NK, NB), 0.4, 2.4, (), jnp.float32)
    det_taps = normal_values(key_list[8], (2, TD), TD ** -0.5, 1.25)
    return {"pieces": pieces, "dest": dest, "offsets": offsets, "kernel_index": kernel_index, "weights": weights, "basis_col": basis_col, "basis_row": basis_row, "coef_table": coef_table, "det_taps": det_taps}


def banded(tap_table, height, columns, center):
    offsets_grid = jnp.arange(columns)[None, :] - jnp.arange(height)[:, None] + center
    one_hot = (offsets_grid[:, :, None] == jnp.arange(tap_table.shape[1])[None, None, :]).astype(jnp.float32)
    return jnp.einsum('ijt,bt->bij', one_hot, tap_table.astype(jnp.float32), precision=lax.Precision.HIGHEST).astype(jnp.bfloat16)


def reference(pieces, dest, offsets, kernel_index, weights, basis_col, basis_row, coef_table, det_taps):
    half_taps = TAPS // 2
    col_bands = banded(basis_col, PW, PW, half_taps).astype(jnp.float32)
    row_bands = banded(basis_row, PR, PR, half_taps).astype(jnp.float32)
    number = pieces.shape[0]
    block_size = math.gcd(number, 64)
    steps_total = number // block_size
    operands = (pieces.reshape(steps_total, block_size, PR, PW), dest[:, 0].reshape(steps_total, block_size),
                offsets.reshape(steps_total, block_size), kernel_index.reshape(steps_total, block_size),
                weights.reshape(steps_total, block_size))

    def accumulate(carry, blocks):
        numerator, denominator = carry
        images, targets, starts, kinds, scales = blocks
        factors = coef_table[kinds]
        stacked = jnp.einsum('nrk,bkc->nbrc', images.astype(jnp.float32), col_bands, precision=lax.Precision.HIGHEST)
        stacked = lax.optimization_barrier(stacked.astype(jnp.bfloat16)).astype(jnp.float32)
        stacked = stacked.reshape(block_size, NB * PR, PW)
        row_kernel = (factors[:, None, :, None] * row_bands.transpose(1, 0, 2)[None]).reshape(block_size, PR, NB * PR)
        row_kernel = lax.optimization_barrier(row_kernel.astype(jnp.bfloat16)).astype(jnp.float32)
        matched = jnp.einsum('nrq,nqc->nrc', row_kernel, stacked, precision=lax.Precision.HIGHEST)
        matched = lax.optimization_barrier(matched.astype(jnp.bfloat16)).astype(jnp.float32)
        scale_float = scales.astype(jnp.float32)
        terms = (scale_float[:, None, None] * matched).reshape(block_size * PR, PW)
        row_index = (targets[:, None] * PH + starts[:, None] + jnp.arange(PR)[None, :]).reshape(-1).astype(jnp.int32)
        numerator = numerator.at[row_index].add(terms)
        denominator = denominator.at[row_index].add(jnp.repeat(scale_float, PR))
        return (numerator, denominator), None

    start_carry = (jnp.zeros((N_PATCH * PH, PW), jnp.float32), jnp.zeros((N_PATCH * PH,), jnp.float32))
    (numerator, denominator), _ = lax.scan(accumulate, start_carry, operands)
    coadd = numerator / (1.0 + denominator)[:, None]
    det_half = TD // 2
    det_cols = banded(det_taps[1:2], PW, PW, det_half)[0]
    det_rows = banded(det_taps[0:1], PH, PH, det_half)[0].astype(jnp.float32)
    coadd_low = coadd.astype(jnp.bfloat16)
    smoothed = jnp.dot(coadd_low, det_cols, preferred_element_type=jnp.float32).astype(jnp.bfloat16)
    smoothed = smoothed.astype(jnp.float32).reshape(N_PATCH, PH, PW)
    detection = jnp.einsum('rs,psc->prc', det_rows, smoothed, precision=lax.Precision.HIGHEST).reshape(N_PATCH * PH, PW)
    return coadd, detection
```

```python
import functools

import jax
import jax.numpy as jnp
from jax import lax
from jax.experimental import pallas as pl
from jax.experimental.pallas import tpu as pltpu
from jax.sharding import PartitionSpec as P

MESH = pl.DeviceIdType.MESH
F32 = jnp.float32
BF16 = jnp.bfloat16

PIECES = 96
PR = 32
PW = 128
PH = 256
TAPS = 41
NB = 14
TD = 21
SIDE = 8
VISITS = 4
GROUP = 16
STRIP = PH // VISITS
HALO = 16
CHUNKS = 2
CHUNK_SLOTS = 16 // CHUNKS
CHUNK_DESTS = 8 // CHUNKS


def iota(shape, axis):
    return lax.broadcasted_iota(jnp.int32, shape, axis)


def match_kernel(
    dest_s, off_s, kind_s, weight_s, coef_s, col_ref, row_ref, x_ref,
    data_ref, meta_ref,
    g_ref, r_ref, y_ref, pad_ref, mt_ref, mw_ref, count_s,
):
    half = TAPS // 2
    pad_ref[...] = jnp.zeros_like(pad_ref)
    pad_ref[0:NB, 4 : 4 + TAPS] = col_ref[...].astype(F32)
    pad_ref[16 : 16 + NB, 4 : 4 + TAPS] = row_ref[...].astype(F32)
    band = jnp.abs(iota((PW, PW), 1) - iota((PW, PW), 0)) <= half
    row_lane = iota((PR, PW), 1)
    row_band = (jnp.abs(row_lane - iota((PR, PW), 0)) <= half) & (row_lane < PR)
    for b in range(NB):
        taps = jnp.broadcast_to(pad_ref[b : b + 1, :], (PW, PW))
        g = pltpu.roll(taps, PW - half - 4, 1, stride=1, stride_axis=0)
        g_ref[b * PW : (b + 1) * PW, :] = jnp.where(band, g, 0.0).astype(BF16)
        taps = jnp.broadcast_to(pad_ref[16 + b : 17 + b, :], (PR, PW))
        r = pltpu.roll(taps, PW - half - 4, 1, stride=1, stride_axis=0)
        r = jnp.where(row_band, r, 0.0)
        r = r + pltpu.roll(r, 32, 1) + pltpu.roll(r, 64, 1) + pltpu.roll(r, 96, 1)
        r_ref[b] = r.reshape(4, 8, PW)

    data_ref[...] = jnp.zeros_like(data_ref)
    mt_ref[...] = jnp.zeros_like(mt_ref)
    mw_ref[...] = jnp.zeros_like(mw_ref)

    @pl.loop(0, 128)
    def _(d):
        count_s[d] = 0

    lane8 = iota((8, PW), 1)
    lane1 = iota((1, PW), 1)
    step = (lane1 % 32).astype(F32)
    which = (lane1 // 32) % 2
    zeros = jnp.zeros((PR, PW), BF16)

    @pl.loop(0, PIECES // GROUP)
    def _(group):
        first = group * GROUP
        for quad in range(GROUP // 4):
            kinds = [kind_s[first + quad * 4 + j] for j in range(4)]
            parts = []
            for b in range(NB):
                factor = jnp.where(
                    lane8 < 64,
                    jnp.where(lane8 < 32, coef_s[kinds[0], b], coef_s[kinds[1], b]),
                    jnp.where(lane8 < 96, coef_s[kinds[2], b], coef_s[kinds[3], b]),
                )
                parts.append((r_ref[b] * factor[None]).reshape(PR, PW))
            row_kernel = jnp.concatenate(parts, axis=0).astype(BF16)
            x = [x_ref[first + quad * 4 + j] for j in range(4)]
            for pair in range(2):
                rows = []
                for j in range(4):
                    left = x[j] if j == 2 * pair else zeros
                    right = x[j] if j == 2 * pair + 1 else zeros
                    rows.append(jnp.concatenate([left, right], axis=1))
                both = jnp.concatenate(rows, axis=0)
                y = jnp.dot(row_kernel, both, preferred_element_type=F32).astype(BF16)
                for j in range(2):
                    at = (quad * 4 + pair * 2 + j) * PR
                    for b in range(NB):
                        y_ref[at : at + PR, b * PW : (b + 1) * PW] = y[
                            b * PR : (b + 1) * PR, j * PW : (j + 1) * PW
                        ]
        matched = jnp.dot(y_ref[...], g_ref[...], preferred_element_type=F32).astype(BF16)
        for j in range(GROUP):
            n = first + j
            d = dest_s[n]
            k = count_s[d]
            count_s[d] = k + 1
            y_to = d // 16
            z_to = (d // 2) % 8
            c_to = d % 2
            message = jnp.where(c_to == 0, z_to, 8 + y_to)
            inner = jnp.where(c_to == 0, y_to, z_to)
            row = message * 8 + inner
            data_ref[row * 2 + k] = matched[j * PR : (j + 1) * PR, :]
            mine = which == k
            mt_ref[pl.ds(row, 1), :] = jnp.where(
                mine, off_s[n].astype(F32) + step, mt_ref[pl.ds(row, 1), :]
            )
            mw_ref[pl.ds(row, 1), :] = jnp.where(mine, weight_s[n], mw_ref[pl.ds(row, 1), :])

    meta_ref[...] = jnp.concatenate(
        [mt_ref[...].reshape(16, 8, PW), mw_ref[...].reshape(16, 8, PW)], axis=1
    ).astype(BF16)


def exchange_kernel(
    data_ref, meta_ref, taps_ref,
    coadd_ref, detection_ref,
    rb, mb, mf, sb, rbb, sc, rc, den_ref, pad_ref, d_ref, f_ref,
    meta_send, meta_recv, a_send, a_recv, b_send, b_recv, c_send, c_recv,
):
    p = lax.axis_index("patch")
    v = lax.axis_index("visit")
    c = lax.rem(p, 2)
    z = lax.rem(p // 2, SIDE)
    y = p // (2 * SIDE)
    along = jnp.where(c == 0, y, z)

    def patch_of(y_at, z_at, c_at):
        return (y_at * SIDE + z_at) * 2 + c_at

    barrier = pltpu.get_barrier_semaphore()

    def greet(target):
        pl.semaphore_signal(barrier, inc=1, device_id={"patch": target}, device_id_type=MESH)

    @pl.loop(1, SIDE)
    def _(i):
        for core in range(2):
            greet(patch_of(y, lax.rem(z + i, SIDE), core))
            greet(patch_of(lax.rem(y + i, SIDE), z, core))

    greet(patch_of(y, z, 1 - c))

    @pl.loop(1, VISITS)
    def _(i):
        pl.semaphore_signal(
            barrier, inc=1, device_id={"visit": lax.rem(v + i, VISITS)}, device_id_type=MESH
        )

    half = TD // 2
    pad_ref[...] = jnp.zeros_like(pad_ref)
    pad_ref[0:2, 6 : 6 + TD] = taps_ref[...].astype(F32)
    cols = pltpu.roll(jnp.broadcast_to(pad_ref[1:2, :], (PW, PW)), PW - half - 6, 1, stride=1, stride_axis=0)
    d_ref[...] = jnp.where(
        jnp.abs(iota((PW, PW), 1) - iota((PW, PW), 0)) <= half, cols, 0.0
    ).astype(BF16)
    rows = pltpu.roll(
        jnp.broadcast_to(pad_ref[0:1, :], (STRIP, PW)), HALO - half - 6, 1, stride=1, stride_axis=0
    )
    f_ref[...] = rows.astype(BF16)

    pl.semaphore_wait(barrier, 4 * (SIDE - 1) + 1 + VISITS - 1)

    def meta_copy(message, slot, target):
        return pltpu.make_async_remote_copy(
            src_ref=meta_ref.at[message], dst_ref=mb.at[slot],
            send_sem=meta_send.at[message], recv_sem=meta_recv.at[slot],
            device_id={"patch": target}, device_id_type=MESH,
        )

    def chunk_of(message, part):
        return data_ref.at[pl.ds(message * 16 + part * CHUNK_SLOTS, CHUNK_SLOTS)]

    def slots_of(slot, part):
        return rb.at[slot, pl.ds(part * CHUNK_SLOTS, CHUNK_SLOTS)]

    def a_copy(message, part, slot, target):
        return pltpu.make_async_remote_copy(
            src_ref=chunk_of(message, part), dst_ref=slots_of(slot, part),
            send_sem=a_send.at[part, message], recv_sem=a_recv.at[part, slot],
            device_id={"patch": target}, device_id_type=MESH,
        )

    z_slot = z * 2 + c
    y_slot = y * 2 + c
    here = jnp.where(c == 0, z, 8 + y)
    here_slot = jnp.where(c == 0, z_slot, y_slot)
    other = jnp.where(c == 0, 8 + y, z)
    other_slot = jnp.where(c == 0, y_slot, z_slot)
    partner = patch_of(y, z, 1 - c)

    pltpu.make_async_copy(meta_ref.at[here], mb.at[here_slot], meta_recv.at[here_slot]).start()
    meta_copy(other, other_slot, partner).start()

    @pl.loop(1, SIDE)
    def _(i):
        z_to = lax.rem(z + i, SIDE)
        y_to = lax.rem(y + i, SIDE)
        meta_copy(z_to, z_slot, patch_of(y, z_to, 0)).start()
        meta_copy(8 + y_to, y_slot, patch_of(y_to, z, 1)).start()

    for part in range(CHUNKS):

        @pl.loop(1, SIDE)
        def _(i):
            z_to = lax.rem(z + i, SIDE)
            y_to = lax.rem(y + i, SIDE)
            a_copy(z_to, part, z_slot, patch_of(y, z_to, 0)).start()
            a_copy(8 + y_to, part, y_slot, patch_of(y_to, z, 1)).start()

        a_copy(other, part, other_slot, partner).start()
        pltpu.make_async_copy(
            chunk_of(here, part), slots_of(here_slot, part), a_recv.at[part, here_slot]
        ).start()

    @pl.loop(0, 16)
    def _(s):
        meta_copy(s, s, partner).wait_recv()

    mf[...] = mb[...].astype(F32)

    row_f = iota((PH, PW), 0).astype(F32)
    low = iota((1, PW), 1) < 64
    eye = iota((PW, PW), 0) == iota((PW, PW), 1)
    tile_row = iota((16, PW), 0)
    ones = jnp.ones((4 * 64, PW), BF16)

    def b_copy(j):
        return pltpu.make_async_remote_copy(
            src_ref=sb.at[j], dst_ref=rbb.at[along],
            send_sem=b_send.at[j], recv_sem=b_recv.at[along],
            device_id={"patch": jnp.where(c == 0, patch_of(j, z, 0), patch_of(y, j, 1))},
            device_id_type=MESH,
        )

    for part in range(CHUNKS):

        @pl.loop(0, 16)
        def _(s):
            a_copy(s, part, s, partner).wait_recv()

        @pl.loop(part * CHUNK_DESTS, (part + 1) * CHUNK_DESTS)
        def _(j):
            total = jnp.zeros((PH, 2 * PW), F32)
            for four in range(4):
                places = []
                blocks = []
                for pair in range(2):
                    s = four * 4 + pair * 2
                    t = jnp.where(low, mf[s, pl.ds(j, 1), :], mf[s + 1, pl.ds(j, 1), :])
                    w = jnp.where(low, mf[s, pl.ds(8 + j, 1), :], mf[s + 1, pl.ds(8 + j, 1), :])
                    places.append(jnp.where(row_f == t, w, 0.0).astype(BF16))
                    for k in range(2):
                        blocks.append(rb[s + k, pl.ds(2 * j, 2)].reshape(64, PW))
                place = jnp.concatenate(places, axis=1)
                block = jnp.concatenate([jnp.concatenate(blocks, axis=0), ones], axis=1)
                total = total + jnp.dot(place, block, preferred_element_type=F32)
            sb[j, 0:PH, :] = total[:, 0:PW].astype(BF16)
            d0 = jnp.sum(jnp.where(eye, total[0:PW, PW:], 0.0), axis=0, keepdims=True)
            d1 = jnp.sum(jnp.where(eye, total[PW:, PW:], 0.0), axis=0, keepdims=True)
            h0 = d0.astype(BF16).astype(F32)
            h1 = d1.astype(BF16).astype(F32)
            tile = jnp.where(tile_row == 0, h0, jnp.where(tile_row == 1, h1, 0.0))
            tile = jnp.where(tile_row == 8, d0 - h0, jnp.where(tile_row == 9, d1 - h1, tile))
            sb[j, PH : PH + 16, :] = tile.astype(BF16)

            @pl.when(j == along)
            def _():
                pltpu.make_async_copy(sb.at[j], rbb.at[along], b_recv.at[along]).start()

            @pl.when(j != along)
            def _():
                b_copy(j).start()

    num = jnp.zeros((PH, PW), F32)
    den = jnp.zeros((8, PW), F32)
    for i in range(SIDE):
        pltpu.make_async_copy(rbb.at[i], rbb.at[i], b_recv.at[i]).wait()
        num = num + rbb[i, 0:PH, :].astype(F32)
        tile = rbb[i, PH : PH + 16, :].astype(F32)
        den = den + (tile[0:8] + tile[8:16])

    edge = jnp.zeros((HALO, PW), F32)
    for x in range(VISITS):
        start = x * STRIP - HALO
        stop = start + STRIP + 2 * HALO
        if x == 0:
            strip = jnp.concatenate([edge, num[0:stop]], axis=0)
        elif x == VISITS - 1:
            strip = jnp.concatenate([num[start:PH], edge], axis=0)
        else:
            strip = num[start:stop]
        sc[x, 0 : STRIP + 2 * HALO, :] = strip
        sc[x, STRIP + 2 * HALO :, :] = den

    def c_copy(x):
        return pltpu.make_async_remote_copy(
            src_ref=sc.at[x], dst_ref=rc.at[v], send_sem=c_send.at[x], recv_sem=c_recv.at[v],
            device_id={"visit": x}, device_id_type=MESH,
        )

    @pl.loop(1, VISITS)
    def _(i):
        c_copy(lax.rem(v + i, VISITS)).start()

    pltpu.make_async_copy(sc.at[v], rc.at[v], c_recv.at[v]).start()

    total = jnp.zeros((STRIP + 2 * HALO, PW), F32)
    den = jnp.zeros((8, PW), F32)
    for i in range(VISITS):
        pltpu.make_async_copy(rc.at[i], rc.at[i], c_recv.at[i]).wait()
        total = total + rc[i, 0 : STRIP + 2 * HALO, :]
        den = den + rc[i, STRIP + 2 * HALO :, :]

    den_ref[...] = jnp.zeros_like(den_ref)
    for a in range(2):
        spread = jnp.where(eye, jnp.broadcast_to(den[a : a + 1, :], (PW, PW)), 0.0)
        column = jnp.sum(spread, axis=1, keepdims=True)
        den_ref[HALO + a * PW : HALO + (a + 1) * PW, :] = jnp.broadcast_to(column, (PW, PW))
    mine = den_ref[pl.ds(pl.multiple_of(v * STRIP, STRIP), STRIP + 2 * HALO), :]
    coadd = total / (1.0 + mine)
    coadd_ref[...] = coadd[HALO : HALO + STRIP]
    smoothed = jnp.dot(coadd.astype(BF16), d_ref[...], preferred_element_type=F32).astype(BF16)
    smoothed = jnp.concatenate([smoothed, jnp.zeros((PW - STRIP - 2 * HALO, PW), BF16)], axis=0)
    detection_ref[...] = jnp.dot(f_ref[...], smoothed, preferred_element_type=F32)

    meta_copy(other, other_slot, partner).wait_send()

    @pl.loop(1, SIDE)
    def _(i):
        meta_copy(lax.rem(z + i, SIDE), z_slot, partner).wait_send()
        meta_copy(8 + lax.rem(y + i, SIDE), y_slot, partner).wait_send()

    for part in range(CHUNKS):
        a_copy(other, part, other_slot, partner).wait_send()

        @pl.loop(1, SIDE)
        def _(i):
            a_copy(lax.rem(z + i, SIDE), part, z_slot, partner).wait_send()
            a_copy(8 + lax.rem(y + i, SIDE), part, y_slot, partner).wait_send()

    @pl.loop(0, SIDE)
    def _(j):
        @pl.when(j != along)
        def _():
            b_copy(j).wait_send()

    @pl.loop(1, VISITS)
    def _(i):
        c_copy(lax.rem(v + i, VISITS)).wait_send()


def match(pieces, dest, offsets, kernel_index, weights, basis_col, basis_row, coef_table):
    smem = pl.BlockSpec(memory_space=pltpu.SMEM)
    vmem = pl.BlockSpec(memory_space=pltpu.VMEM)
    return pl.pallas_call(
        match_kernel,
        out_shape=(
            jax.ShapeDtypeStruct((256, PR, PW), BF16),
            jax.ShapeDtypeStruct((16, 16, PW), BF16),
        ),
        in_specs=[smem] * 5 + [vmem] * 3,
        out_specs=(vmem, vmem),
        scratch_shapes=[
            pltpu.VMEM((NB * PW, PW), BF16),
            pltpu.VMEM((NB, 4, 8, PW), F32),
            pltpu.VMEM((GROUP * PR, NB * PW), BF16),
            pltpu.VMEM((32, PW), F32),
            pltpu.VMEM((128, PW), F32),
            pltpu.VMEM((128, PW), F32),
            pltpu.SMEM((128,), jnp.int32),
        ],
        name="match",
    )(dest[:, 0], offsets, kernel_index, weights.astype(F32), coef_table, basis_col, basis_row, pieces)


def exchange(data, meta, det_taps):
    hbm = pl.BlockSpec(memory_space=pl.ANY)
    vmem = pl.BlockSpec(memory_space=pltpu.VMEM)
    dma = pltpu.SemaphoreType.DMA
    out = jax.ShapeDtypeStruct((STRIP, PW), F32)
    return pl.pallas_call(
        exchange_kernel,
        out_shape=(out, out),
        in_specs=[hbm, hbm, vmem],
        out_specs=(vmem, vmem),
        scratch_shapes=[
            pltpu.VMEM((16, 16, PR, PW), BF16),
            pltpu.VMEM((16, 16, PW), BF16),
            pltpu.VMEM((16, 16, PW), F32),
            pltpu.VMEM((SIDE, PH + 16, PW), BF16),
            pltpu.VMEM((SIDE, PH + 16, PW), BF16),
            pltpu.VMEM((VISITS, STRIP + 2 * HALO + 8, PW), F32),
            pltpu.VMEM((VISITS, STRIP + 2 * HALO + 8, PW), F32),
            pltpu.VMEM((PH + 2 * HALO, PW), F32),
            pltpu.VMEM((8, PW), F32),
            pltpu.VMEM((PW, PW), BF16),
            pltpu.VMEM((STRIP, PW), BF16),
            dma((16,)),
            dma((16,)),
            dma((CHUNKS, 16)),
            dma((CHUNKS, 16)),
            dma((SIDE,)),
            dma((SIDE,)),
            dma((VISITS,)),
            dma((VISITS,)),
        ],
        compiler_params=pltpu.CompilerParams(collective_id=0, has_side_effects=True),
        name="exchange",
    )(data, meta, det_taps)


def shards(
    pieces, dest, offsets, kernel_index, weights, basis_col, basis_row, coef_table, det_taps
):
    data, meta = match(
        pieces, dest, offsets, kernel_index, weights, basis_col, basis_row, coef_table
    )
    return exchange(data, meta, det_taps)


def solution(mesh):
    split = P(("patch", "visit"))
    in_specs = (
        P(("patch", "visit"), None, None),
        P(("patch", "visit"), None),
        split,
        split,
        split,
        P(),
        P(),
        P(),
        P(),
    )
    out_specs = (P(("patch", "visit"), None), P(("patch", "visit"), None))
    return jax.shard_map(shards, mesh=mesh, in_specs=in_specs, out_specs=out_specs, check_vma=False)
```

```python
import functools

import jax
import jax.numpy as jnp
from jax import lax
from jax.experimental import pallas as pl
from jax.experimental.pallas import tpu as pltpu
from jax.sharding import PartitionSpec as P

MESH = pl.DeviceIdType.MESH
F32 = jnp.float32
BF16 = jnp.bfloat16
I32 = jnp.int32

PIECES = 96
PR = 32
PW = 128
PH = 256
TAPS = 41
NB = 14
TD = 21
SIDE = 8
VISITS = 4
GROUP = 16
STRIP = PH // VISITS
HALO = 16
SPAN = STRIP + 2 * HALO
SLOTS = 16
META = 16
ROWS = META + SLOTS * PR
CHUNKS = 2
CHUNK_DESTS = 8 // CHUNKS
ORDER = (3, 5, 4, 2, 6, 1, 7, 0)


def iota(shape, axis):
    return lax.broadcasted_iota(I32, shape, axis)


def chosen(index, values):
    result = jnp.full_like(index, values[-1])
    for at, value in enumerate(values[:-1]):
        result = jnp.where(index == at, value, result)
    return result


def tables(col_ref, row_ref, pad_ref, g_ref, r_ref):
    half = TAPS // 2
    pad_ref[...] = jnp.zeros_like(pad_ref)
    pad_ref[0:NB, 4 : 4 + TAPS] = col_ref[...].astype(F32)
    pad_ref[16 : 16 + NB, 4 : 4 + TAPS] = row_ref[...].astype(F32)
    band = jnp.abs(iota((PW, PW), 1) - iota((PW, PW), 0)) <= half
    row_lane = iota((PR, PW), 1)
    row_band = (jnp.abs(row_lane - iota((PR, PW), 0)) <= half) & (row_lane < PR)
    for b in range(NB):
        taps = jnp.broadcast_to(pad_ref[b : b + 1, :], (PW, PW))
        g = pltpu.roll(taps, PW - half - 4, 1, stride=1, stride_axis=0)
        g_ref[b * PW : (b + 1) * PW, :] = jnp.where(band, g, 0.0).astype(BF16)
        taps = jnp.broadcast_to(pad_ref[16 + b : 17 + b, :], (PR, PW))
        r = pltpu.roll(taps, PW - half - 4, 1, stride=1, stride_axis=0)
        r = jnp.where(row_band, r, 0.0)
        r = r + pltpu.roll(r, 32, 1) + pltpu.roll(r, 64, 1) + pltpu.roll(r, 96, 1)
        r_ref[b] = r.reshape(4, 8, PW)


def plan(y, z, dest_ref, off_ref, weight_ref, plan_ref, padf_ref, stage_ref):
    plan_ref[...] = jnp.full_like(plan_ref, -1)
    plan_ref[0:1, 0:PIECES] = dest_ref[...]
    padf_ref[...] = jnp.zeros_like(padf_ref)
    padf_ref[0:1, 0:PIECES] = off_ref[...].astype(F32)
    padf_ref[1:2, 0:PIECES] = weight_ref[...].astype(F32)
    square = (PW, PW)
    lane, row = iota(square, 1), iota(square, 0)
    d = jnp.broadcast_to(plan_ref[0:1, :], square)
    d_t = d.T
    earlier = jnp.sum(jnp.where((d == d_t) & (row < lane), 1, 0), axis=0, keepdims=True)
    d1 = plan_ref[0:1, :]
    y_to, z_to, c_to = d1 >> 4, (d1 >> 1) & 7, d1 & 1
    distance = jnp.where(c_to == 0, z_to - z, y_to - y) & 7
    inner = jnp.where(c_to == 0, y_to, z_to)
    turn = chosen(distance, tuple(ORDER.index(o) for o in range(SIDE)))
    position = ((turn * 2 + c_to) * 8 + inner) * 2 + earlier
    lane1 = iota((1, PW), 1)
    position = jnp.where(lane1 < PIECES, position, 1024 + lane1)
    pos = jnp.broadcast_to(position, square)
    pos_t = pos.T
    rank = jnp.sum(jnp.where(pos_t < pos, 1, 0), axis=0, keepdims=True)
    rank_t = jnp.broadcast_to(rank, square).T
    order = jnp.sum(jnp.where(rank_t == lane, row, 0), axis=0, keepdims=True)
    plan_ref[0:1, :] = order
    for a in range(2):
        plan_ref[1 + a : 2 + a, :] = PIECES + jnp.sum(
            jnp.where(pos_t == lane + a * PW, rank_t - PIECES, 0), axis=0, keepdims=True
        )
    which = (lane // PR) & 1
    hot = jnp.concatenate(
        [jnp.where(pos == 2 * row + k, 1.0, 0.0).astype(BF16) for k in range(2)], axis=1
    )
    found = []
    for at in range(2):
        value = jnp.broadcast_to(padf_ref[at : at + 1, :], square).T
        value = jnp.concatenate(
            [jnp.where(which == k, value, 0.0).astype(BF16) for k in range(2)], axis=0
        )
        found.append(jnp.dot(hot, value, preferred_element_type=F32))
    target = found[0] + (lane & (PR - 1)).astype(F32)
    stage_ref[:, 0:META, :] = jnp.concatenate(
        [target.reshape(16, 8, PW), found[1].reshape(16, 8, PW)], axis=1
    ).astype(BF16)


def match_group(group, kind_s, coef_s, plan_s, x, r_ref, g_ref, y_ref, matched_ref):
    first = group * GROUP
    lane8 = iota((8, PW), 1)
    zeros = jnp.zeros((PR, PW), BF16)
    for quad in range(GROUP // 4):
        pieces = [plan_s[0, first + quad * 4 + j] for j in range(4)]
        kinds = [kind_s[n] for n in pieces]
        parts = []
        for b in range(NB):
            factor = jnp.where(
                lane8 < 64,
                jnp.where(lane8 < 32, coef_s[b, kinds[0]], coef_s[b, kinds[1]]),
                jnp.where(lane8 < 96, coef_s[b, kinds[2]], coef_s[b, kinds[3]]),
            )
            parts.append((r_ref[b] * factor[None]).reshape(PR, PW))
        row_kernel = jnp.concatenate(parts, axis=0).astype(BF16)
        images = [x[n] for n in pieces]
        for pair in range(2):
            rows = []
            for j in range(4):
                left = images[j] if j == 2 * pair else zeros
                right = images[j] if j == 2 * pair + 1 else zeros
                rows.append(jnp.concatenate([left, right], axis=1))
            both = jnp.concatenate(rows, axis=0)
            y = jnp.dot(row_kernel, both, preferred_element_type=F32).astype(BF16)
            for j in range(2):
                at = (quad * 4 + pair * 2 + j) * PR
                for b in range(NB):
                    y_ref[at : at + PR, b * PW : (b + 1) * PW] = y[
                        b * PR : (b + 1) * PR, j * PW : (j + 1) * PW
                    ]
    matched = jnp.dot(y_ref[...], g_ref[...], preferred_element_type=F32).astype(BF16)
    matched_ref[pl.ds(first, GROUP)] = matched.reshape(GROUP, PR, PW)


def exchange_kernel(
    kind_s, coef_s, dest_ref, off_ref, weight_ref, col_ref, row_ref, pieces_ref,
    sum_ref,
    x, g_ref, r_ref, y_ref, pad_ref, padf_ref, plan_ref, plan_s, matched_ref, stage_ref,
    rb, mf, sb, rbb, sc, rc,
    x_sem, plan_sem, a_send, a_recv, b_send, b_recv, c_send, c_recv,
):
    p = lax.axis_index("patch")
    v = lax.axis_index("visit")
    c = lax.rem(p, 2)
    z = lax.rem(p // 2, SIDE)
    y = p // (2 * SIDE)
    along = jnp.where(c == 0, y, z)

    def patch_of(y_at, z_at, c_at):
        return (y_at * SIDE + z_at) * 2 + c_at

    x_copy = pltpu.make_async_copy(pieces_ref, x, x_sem)
    x_copy.start()

    barrier = pltpu.get_barrier_semaphore()

    def greet(target):
        pl.semaphore_signal(barrier, inc=1, device_id={"patch": target}, device_id_type=MESH)

    @pl.loop(1, SIDE)
    def _(i):
        for core in range(2):
            greet(patch_of(y, lax.rem(z + i, SIDE), core))
            greet(patch_of(lax.rem(y + i, SIDE), z, core))

    greet(patch_of(y, z, 1 - c))

    @pl.loop(1, VISITS)
    def _(i):
        pl.semaphore_signal(
            barrier, inc=1, device_id={"visit": lax.rem(v + i, VISITS)}, device_id_type=MESH
        )

    plan(y, z, dest_ref, off_ref, weight_ref, plan_ref, padf_ref, stage_ref)
    plan_copy = pltpu.make_async_copy(plan_ref, plan_s, plan_sem)
    plan_copy.start()
    tables(col_ref, row_ref, pad_ref, g_ref, r_ref)
    matched_ref[PIECES:, :, :] = jnp.zeros((8, PR, PW), BF16)
    plan_copy.wait()
    x_copy.wait()

    pl.semaphore_wait(barrier, 4 * (SIDE - 1) + 1 + VISITS - 1)

    def part_of(ref, at, part):
        if part == 0:
            return ref.at[at, pl.ds(0, META + CHUNK_DESTS * 64)]
        return ref.at[at, pl.ds(META + part * CHUNK_DESTS * 64, CHUNK_DESTS * 64)]

    def a_copy(message, part, slot, target):
        return pltpu.make_async_remote_copy(
            src_ref=part_of(stage_ref, message, part), dst_ref=part_of(rb, slot, part),
            send_sem=a_send.at[part, message], recv_sem=a_recv.at[part, slot],
            device_id={"patch": target}, device_id_type=MESH,
        )

    z_slot = z * 2 + c
    y_slot = y * 2 + c
    partner = patch_of(y, z, 1 - c)
    here = 2 * (SIDE - 1) + c

    def fill(message):
        for s in range(SLOTS):
            r = plan_s[1 + message // 8, (message % 8) * SLOTS + s]
            stage_ref[message, META + s * PR : META + (s + 1) * PR, :] = matched_ref[r]

    def send(message, part):
        even = lax.rem(message, 2) == 0
        distance = chosen(message // 2, ORDER)
        target = jnp.where(
            even,
            patch_of(y, lax.rem(z + distance, SIDE), 0),
            patch_of(lax.rem(y + distance, SIDE), z, 1),
        )
        slot = jnp.where(even, z_slot, y_slot)

        @pl.when(message != here)
        def _():
            a_copy(message, part, slot, target).start()

        @pl.when(message == here)
        def _():
            pltpu.make_async_copy(
                part_of(stage_ref, message, part), part_of(rb, slot, part), a_recv.at[part, slot]
            ).start()

    groups = PIECES // GROUP

    @pl.loop(0, groups)
    def _(group):
        match_group(group, kind_s, coef_s, plan_s, x, r_ref, g_ref, y_ref, matched_ref)
        fill(group)
        for part in range(CHUNKS):
            send(group, part)

    @pl.loop(groups, 16)
    def _(message):
        fill(message)
        send(message, 0)

    for part in range(1, CHUNKS):

        @pl.loop(groups, 16)
        def _(message):
            send(message, part)

    row_f = iota((PH, PW), 0).astype(F32)
    low = iota((1, PW), 1) < 64
    eye = iota((PW, PW), 0) == iota((PW, PW), 1)
    tile_row = iota((16, PW), 0)
    ones = jnp.ones((4 * 64, PW), BF16)

    def b_copy(j):
        return pltpu.make_async_remote_copy(
            src_ref=sb.at[j], dst_ref=rbb.at[along],
            send_sem=b_send.at[j], recv_sem=b_recv.at[along],
            device_id={"patch": jnp.where(c == 0, patch_of(j, z, 0), patch_of(y, j, 1))},
            device_id_type=MESH,
        )

    for part in range(CHUNKS):

        @pl.loop(0, 16)
        def _(s):
            a_copy(s, part, s, partner).wait_recv()

        if part == 0:
            mf[...] = rb[:, 0:META, :].astype(F32)

        @pl.loop(part * CHUNK_DESTS, (part + 1) * CHUNK_DESTS)
        def _(j):
            total = jnp.zeros((PH, 2 * PW), F32)
            for four in range(4):
                places = []
                blocks = []
                for pair in range(2):
                    s = four * 4 + pair * 2
                    t = jnp.where(low, mf[s, pl.ds(j, 1), :], mf[s + 1, pl.ds(j, 1), :])
                    w = jnp.where(low, mf[s, pl.ds(8 + j, 1), :], mf[s + 1, pl.ds(8 + j, 1), :])
                    places.append(jnp.where(row_f == t, w, 0.0).astype(BF16))
                    for k in range(2):
                        blocks.append(rb[s + k, pl.ds(pl.multiple_of(META + 64 * j, 16), 64), :])
                place = jnp.concatenate(places, axis=1)
                block = jnp.concatenate([jnp.concatenate(blocks, axis=0), ones], axis=1)
                total = total + jnp.dot(place, block, preferred_element_type=F32)
            sb[j, 0:PH, :] = total[:, 0:PW].astype(BF16)
            d0 = jnp.sum(jnp.where(eye, total[0:PW, PW:], 0.0), axis=0, keepdims=True)
            d1 = jnp.sum(jnp.where(eye, total[PW:, PW:], 0.0), axis=0, keepdims=True)
            h0 = d0.astype(BF16).astype(F32)
            h1 = d1.astype(BF16).astype(F32)
            tile = jnp.where(tile_row == 0, h0, jnp.where(tile_row == 1, h1, 0.0))
            tile = jnp.where(tile_row == 8, d0 - h0, jnp.where(tile_row == 9, d1 - h1, tile))
            sb[j, PH : PH + 16, :] = tile.astype(BF16)

            @pl.when(j == along)
            def _():
                pltpu.make_async_copy(sb.at[j], rbb.at[along], b_recv.at[along]).start()

            @pl.when(j != along)
            def _():
                b_copy(j).start()

    num = jnp.zeros((PH, PW), F32)
    den = jnp.zeros((8, PW), F32)
    for i in range(SIDE):
        pltpu.make_async_copy(rbb.at[i], rbb.at[i], b_recv.at[i]).wait()
        num = num + rbb[i, 0:PH, :].astype(F32)
        tile = rbb[i, PH : PH + 16, :].astype(F32)
        den = den + (tile[0:8] + tile[8:16])

    edge = jnp.zeros((HALO, PW), F32)
    for at in range(VISITS):
        start = at * STRIP - HALO
        stop = start + SPAN
        if at == 0:
            strip = jnp.concatenate([edge, num[0:stop]], axis=0)
        elif at == VISITS - 1:
            strip = jnp.concatenate([num[start:PH], edge], axis=0)
        else:
            strip = num[start:stop]
        sc[at, 0:SPAN, :] = strip
        sc[at, SPAN:, :] = den

    def c_copy(at):
        return pltpu.make_async_remote_copy(
            src_ref=sc.at[at], dst_ref=rc.at[v], send_sem=c_send.at[at], recv_sem=c_recv.at[v],
            device_id={"visit": at}, device_id_type=MESH,
        )

    @pl.loop(1, VISITS)
    def _(i):
        c_copy(lax.rem(v + i, VISITS)).start()

    pltpu.make_async_copy(sc.at[v], rc.at[v], c_recv.at[v]).start()

    for part in range(CHUNKS):

        @pl.loop(0, 16)
        def _(message):
            @pl.when(message != here)
            def _():
                a_copy(message, part, z_slot, partner).wait_send()

    @pl.loop(0, SIDE)
    def _(j):
        @pl.when(j != along)
        def _():
            b_copy(j).wait_send()

    total = jnp.zeros((SPAN + 8, PW), F32)
    for i in range(VISITS):
        pltpu.make_async_copy(rc.at[i], rc.at[i], c_recv.at[i]).wait()
        total = total + rc[i]
    sum_ref[...] = total

    @pl.loop(1, VISITS)
    def _(i):
        c_copy(lax.rem(v + i, VISITS)).wait_send()


def filter_kernel(sum_ref, taps_ref, coadd_ref, detection_ref, den_ref, pad_ref):
    v = lax.axis_index("visit")
    half = TD // 2
    pad_ref[...] = jnp.zeros_like(pad_ref)
    pad_ref[0:2, 6 : 6 + TD] = taps_ref[...].astype(F32)
    square = (PW, PW)
    lane, row = iota(square, 1), iota(square, 0)
    taps = jnp.broadcast_to(pad_ref[1:2, :], square)
    cols = pltpu.roll(taps, PW - half - 6, 1, stride=1, stride_axis=0)
    cols = jnp.where(jnp.abs(lane - row) <= half, cols, 0.0).astype(BF16)
    taps = jnp.broadcast_to(pad_ref[0:1, :], (STRIP, PW))
    rows = pltpu.roll(taps, HALO - half - 6, 1, stride=1, stride_axis=0).astype(BF16)
    den_ref[...] = jnp.zeros_like(den_ref)
    for a in range(2):
        column = jnp.broadcast_to(sum_ref[SPAN + a : SPAN + a + 1, :], square).T
        den_ref[HALO + a * PW : HALO + (a + 1) * PW, :] = column
    den = den_ref[pl.ds(pl.multiple_of(v * STRIP, STRIP), SPAN), :]
    coadd = sum_ref[0:SPAN, :] / (1.0 + den)
    coadd_ref[...] = coadd[HALO : HALO + STRIP]
    smoothed = jnp.dot(coadd.astype(BF16), cols, preferred_element_type=F32).astype(BF16)
    smoothed = jnp.concatenate([smoothed, jnp.zeros((PW - SPAN, PW), BF16)], axis=0)
    detection_ref[...] = jnp.dot(rows, smoothed, preferred_element_type=F32)


SMEM = pl.BlockSpec(memory_space=pltpu.SMEM)
VMEM = pl.BlockSpec(memory_space=pltpu.VMEM)


def exchange(pieces, dest, offsets, kernel_index, weights, basis_col, basis_row, coef_table):
    dma = pltpu.SemaphoreType.DMA
    row = (1, PIECES)
    return pl.pallas_call(
        exchange_kernel,
        out_shape=jax.ShapeDtypeStruct((SPAN + 8, PW), F32),
        in_specs=[SMEM] * 2 + [VMEM] * 5 + [pl.BlockSpec(memory_space=pl.ANY)],
        out_specs=VMEM,
        scratch_shapes=[
            pltpu.VMEM((PIECES, PR, PW), BF16),
            pltpu.VMEM((NB * PW, PW), BF16),
            pltpu.VMEM((NB, 4, 8, PW), F32),
            pltpu.VMEM((GROUP * PR, NB * PW), BF16),
            pltpu.VMEM((32, PW), F32),
            pltpu.VMEM((8, PW), F32),
            pltpu.VMEM((8, PW), I32),
            pltpu.SMEM((8, PW), I32),
            pltpu.VMEM((PIECES + 8, PR, PW), BF16),
            pltpu.VMEM((16, ROWS, PW), BF16),
            pltpu.VMEM((16, ROWS, PW), BF16),
            pltpu.VMEM((16, META, PW), F32),
            pltpu.VMEM((SIDE, PH + 16, PW), BF16),
            pltpu.VMEM((SIDE, PH + 16, PW), BF16),
            pltpu.VMEM((VISITS, SPAN + 8, PW), F32),
            pltpu.VMEM((VISITS, SPAN + 8, PW), F32),
            dma(()),
            dma(()),
            dma((CHUNKS, 16)),
            dma((CHUNKS, 16)),
            dma((SIDE,)),
            dma((SIDE,)),
            dma((VISITS,)),
            dma((VISITS,)),
        ],
        compiler_params=pltpu.CompilerParams(collective_id=0, has_side_effects=True),
        name="exchange",
    )(
        kernel_index, coef_table.T, dest.reshape(row), offsets.reshape(row), weights.reshape(row),
        basis_col, basis_row, pieces,
    )


def finish(sums, det_taps):
    out = jax.ShapeDtypeStruct((STRIP, PW), F32)
    return pl.pallas_call(
        filter_kernel,
        out_shape=(out, out),
        in_specs=[VMEM, VMEM],
        out_specs=(VMEM, VMEM),
        scratch_shapes=[pltpu.VMEM((PH + 2 * HALO, PW), F32), pltpu.VMEM((8, PW), F32)],
        name="finish",
    )(sums, det_taps)


def shards(
    pieces, dest, offsets, kernel_index, weights, basis_col, basis_row, coef_table, det_taps
):
    sums = exchange(
        pieces, dest, offsets, kernel_index, weights, basis_col, basis_row, coef_table
    )
    return finish(sums, det_taps)


def solution(mesh):
    split = P(("patch", "visit"))
    in_specs = (
        P(("patch", "visit"), None, None),
        P(("patch", "visit"), None),
        split,
        split,
        split,
        P(),
        P(),
        P(),
        P(),
    )
    out_specs = (P(("patch", "visit"), None), P(("patch", "visit"), None))
    return jax.shard_map(shards, mesh=mesh, in_specs=in_specs, out_specs=out_specs, check_vma=False)
```

```python
import functools

import jax
import jax.numpy as jnp
from jax import lax
from jax.experimental import pallas as pl
from jax.experimental.pallas import tpu as pltpu
from jax.sharding import PartitionSpec as P

MESH = pl.DeviceIdType.MESH
F32 = jnp.float32
BF16 = jnp.bfloat16
I32 = jnp.int32

PIECES = 96
PR = 32
PW = 128
PH = 256
TAPS = 41
NB = 14
TD = 21
SIDE = 8
VISITS = 4
GROUP = 16
STRIP = PH // VISITS
HALO = 16
SPAN = STRIP + 2 * HALO
CHUNKS = 4
META = 8
DATA = 4 * PR
ROWS = DATA + META
DENSE = PH + 16
ORDER = (3, 2, 5, 4, 6, 1, 7, 0)
FAR = (3, 5, 4)
NEAR = (2, 6, 1, 7, 0)


def iota(shape, axis):
    return lax.broadcasted_iota(I32, shape, axis)


def chosen(index, values):
    result = jnp.full_like(index, values[-1])
    for at, value in enumerate(values[:-1]):
        result = jnp.where(index == at, value, result)
    return result


def tables(col_ref, row_ref, pad_ref, g_ref, r_ref):
    half = TAPS // 2
    pad_ref[...] = jnp.zeros_like(pad_ref)
    pad_ref[0:NB, 4 : 4 + TAPS] = col_ref[...].astype(F32)
    pad_ref[16 : 16 + NB, 4 : 4 + TAPS] = row_ref[...].astype(F32)
    band = jnp.abs(iota((PW, PW), 1) - iota((PW, PW), 0)) <= half
    row_lane = iota((PR, PW), 1)
    row_band = (jnp.abs(row_lane - iota((PR, PW), 0)) <= half) & (row_lane < PR)
    for b in range(NB):
        taps = jnp.broadcast_to(pad_ref[b : b + 1, :], (PW, PW))
        g = pltpu.roll(taps, PW - half - 4, 1, stride=1, stride_axis=0)
        g_ref[b * PW : (b + 1) * PW, :] = jnp.where(band, g, 0.0).astype(BF16)
        taps = jnp.broadcast_to(pad_ref[16 + b : 17 + b, :], (PR, PW))
        r = pltpu.roll(taps, PW - half - 4, 1, stride=1, stride_axis=0)
        r = jnp.where(row_band, r, 0.0)
        r = r + pltpu.roll(r, 32, 1) + pltpu.roll(r, 64, 1) + pltpu.roll(r, 96, 1)
        r_ref[b] = r.reshape(4, 8, PW)


def plan(y, z, dest_ref, off_ref, weight_ref, plan_ref, padf_ref, stage_ref):
    plan_ref[...] = jnp.full_like(plan_ref, -1)
    plan_ref[0:1, 0:PIECES] = dest_ref[...]
    padf_ref[...] = jnp.zeros_like(padf_ref)
    padf_ref[0:1, 0:PIECES] = off_ref[...].astype(F32)
    padf_ref[1:2, 0:PIECES] = weight_ref[...].astype(F32)
    square = (PW, PW)
    lane, row = iota(square, 1), iota(square, 0)
    d = jnp.broadcast_to(plan_ref[0:1, :], square)
    d_t = d.T
    earlier = jnp.sum(jnp.where((d == d_t) & (row < lane), 1, 0), axis=0, keepdims=True)
    d1 = plan_ref[0:1, :]
    y_to, z_to, c_to = d1 >> 4, (d1 >> 1) & 7, d1 & 1
    distance = jnp.where(c_to == 0, z_to - z, y_to - y) & 7
    inner = jnp.where(c_to == 0, y_to, z_to)
    turn = chosen(distance, tuple(ORDER.index(o) for o in range(SIDE)))
    position = ((turn * 2 + c_to) * 8 + inner) * 2 + earlier
    lane1 = iota((1, PW), 1)
    position = jnp.where(lane1 < PIECES, position, 1024 + lane1)
    pos = jnp.broadcast_to(position, square)
    pos_t = pos.T
    rank = jnp.sum(jnp.where(pos_t < pos, 1, 0), axis=0, keepdims=True)
    rank_t = jnp.broadcast_to(rank, square).T
    order = jnp.sum(jnp.where(rank_t == lane, row, 0), axis=0, keepdims=True)
    plan_ref[0:1, :] = order
    for a in range(2):
        plan_ref[1 + a : 2 + a, :] = PIECES + jnp.sum(
            jnp.where(pos_t == lane + a * PW, rank_t - PIECES, 0), axis=0, keepdims=True
        )
    shape = (16 * CHUNKS * META, PW)
    line = iota(shape, 0)
    wanted = ((line // META) * 2 + (line & 1)) * 2
    spots = jnp.broadcast_to(position, shape)
    hot = jnp.concatenate(
        [jnp.where(spots == wanted + k, 1.0, 0.0).astype(BF16) for k in range(2)], axis=1
    )
    which = (lane // PR) & 1
    values = []
    for at in range(2):
        value = jnp.broadcast_to(padf_ref[at : at + 1, :], square).T
        values.append(
            jnp.concatenate(
                [jnp.where(which == k, value, 0.0).astype(BF16) for k in range(2)], axis=0
            )
        )
    found = jnp.dot(hot, jnp.concatenate(values, axis=1), preferred_element_type=F32)
    target = found[:, 0:PW] + (iota(shape, 1) & (PR - 1)).astype(F32)
    both = jnp.where((line & 4) == 0, target, found[:, PW:])
    stage_ref[:, :, DATA:, :] = both.reshape(16, CHUNKS, META, PW).astype(BF16)


def match_group(group, kind_s, coef_s, plan_s, x, r_ref, g_ref, y_ref, matched_ref):
    first = group * GROUP
    lane8 = iota((8, PW), 1)
    zeros = jnp.zeros((PR, PW), BF16)
    for quad in range(GROUP // 4):
        pieces = [plan_s[0, first + quad * 4 + j] for j in range(4)]
        kinds = [kind_s[n] for n in pieces]
        parts = []
        for b in range(NB):
            factor = jnp.where(
                lane8 < 64,
                jnp.where(lane8 < 32, coef_s[b, kinds[0]], coef_s[b, kinds[1]]),
                jnp.where(lane8 < 96, coef_s[b, kinds[2]], coef_s[b, kinds[3]]),
            )
            parts.append((r_ref[b] * factor[None]).reshape(PR, PW))
        row_kernel = jnp.concatenate(parts, axis=0).astype(BF16)
        images = [x[n] for n in pieces]
        for pair in range(2):
            rows = []
            for j in range(4):
                left = images[j] if j == 2 * pair else zeros
                right = images[j] if j == 2 * pair + 1 else zeros
                rows.append(jnp.concatenate([left, right], axis=1))
            both = jnp.concatenate(rows, axis=0)
            y = jnp.dot(row_kernel, both, preferred_element_type=F32).astype(BF16)
            for j in range(2):
                at = (quad * 4 + pair * 2 + j) * PR
                for b in range(NB):
                    y_ref[at : at + PR, b * PW : (b + 1) * PW] = y[
                        b * PR : (b + 1) * PR, j * PW : (j + 1) * PW
                    ]
    matched = jnp.dot(y_ref[...], g_ref[...], preferred_element_type=F32).astype(BF16)
    matched_ref[pl.ds(first, GROUP)] = matched.reshape(GROUP, PR, PW)


def exchange_kernel(
    kind_s, coef_s, dest_ref, off_ref, weight_ref, col_ref, row_ref, pieces_ref,
    sum_ref,
    x, g_ref, r_ref, y_ref, pad_ref, padf_ref, plan_ref, plan_s, matched_ref, stage_ref,
    rb, rf, mf, fd, rd, sb, rbb, sc, rc,
    x_sem, plan_sem, a_send, a_recv, f_recv, d_send, d_recv, b_send, b_recv, c_send, c_recv,
):
    p = lax.axis_index("patch")
    v = lax.axis_index("visit")
    c = lax.rem(p, 2)
    z = lax.rem(p // 2, SIDE)
    y = p // (2 * SIDE)
    along = jnp.where(c == 0, y, z)

    def patch_of(y_at, z_at, c_at):
        return (y_at * SIDE + z_at) * 2 + c_at

    x_copy = pltpu.make_async_copy(pieces_ref, x, x_sem)
    x_copy.start()

    barrier = pltpu.get_barrier_semaphore()

    def greet(target):
        pl.semaphore_signal(barrier, inc=1, device_id={"patch": target}, device_id_type=MESH)

    @pl.loop(1, SIDE)
    def _(i):
        for core in range(2):
            greet(patch_of(y, lax.rem(z + i, SIDE), core))
            greet(patch_of(lax.rem(y + i, SIDE), z, core))

    greet(patch_of(y, z, 1 - c))

    @pl.loop(1, VISITS)
    def _(i):
        for core in range(2):
            pl.semaphore_signal(
                barrier, inc=1,
                device_id={"patch": patch_of(y, z, core), "visit": lax.rem(v + i, VISITS)},
                device_id_type=MESH,
            )

    plan(y, z, dest_ref, off_ref, weight_ref, plan_ref, padf_ref, stage_ref)
    plan_copy = pltpu.make_async_copy(plan_ref, plan_s, plan_sem)
    plan_copy.start()
    tables(col_ref, row_ref, pad_ref, g_ref, r_ref)
    matched_ref[PIECES:, :, :] = jnp.zeros((8, PR, PW), BF16)
    plan_copy.wait()
    x_copy.wait()

    pl.semaphore_wait(barrier, 4 * (SIDE - 1) + 1 + 2 * (VISITS - 1))

    partner = patch_of(y, z, 1 - c)

    def near_copy(message, part, slot, target):
        return pltpu.make_async_remote_copy(
            src_ref=stage_ref.at[message, part], dst_ref=rb.at[slot, part],
            send_sem=a_send.at[message, part], recv_sem=a_recv.at[slot, part],
            device_id={"patch": target}, device_id_type=MESH,
        )

    def far_copy(message, part, index, target):
        slot = v * 2 + c
        return pltpu.make_async_remote_copy(
            src_ref=stage_ref.at[message, part], dst_ref=rf.at[index, slot],
            send_sem=a_send.at[message, part], recv_sem=f_recv.at[index, slot],
            device_id={"patch": target, "visit": part}, device_id_type=MESH,
        )

    def fill(message):
        for s in range(16):
            r = plan_s[1 + message // 8, (message % 8) * 16 + s]
            stage_ref[message, s // 4, (s % 4) * PR : (s % 4 + 1) * PR, :] = matched_ref[r]

    def turn_part(turn):
        return lax.rem(v + 1 + turn, VISITS)

    def send_near(message, part):
        turn = message // 2
        core = lax.rem(message, 2)
        distance = chosen(turn, ORDER)
        slot = chosen(turn, tuple(max(0, NEAR.index(o) if o in NEAR else 0) for o in ORDER)) * 2 + c
        target = jnp.where(
            core == 0,
            patch_of(y, lax.rem(z + distance, SIDE), 0),
            patch_of(lax.rem(y + distance, SIDE), z, 1),
        )
        here = (distance == 0) & (core == c)

        @pl.when(jnp.logical_not(here))
        def _():
            near_copy(message, part, slot, target).start()

        @pl.when(here)
        def _():
            pltpu.make_async_copy(
                stage_ref.at[message, part], rb.at[slot, part], a_recv.at[slot, part]
            ).start()

    def send_far(message, part):
        core = lax.rem(message, 2)
        index = chosen(message // 2, tuple(FAR.index(o) if o in FAR else 0 for o in ORDER))
        here = (part == v) & (core == c)

        @pl.when(jnp.logical_not(here))
        def _():
            far_copy(message, part, index, patch_of(y, z, core)).start()

        @pl.when(here)
        def _():
            slot = v * 2 + c
            pltpu.make_async_copy(
                stage_ref.at[message, part], rf.at[index, slot], f_recv.at[index, slot]
            ).start()

    row_f = iota((PH, PW), 0).astype(F32)
    low = iota((1, PW), 1) < 64
    eye = iota((PW, PW), 0) == iota((PW, PW), 1)
    tile_row = iota((16, PW), 0)

    def add_up(count, e, load):
        places = []
        blocks = []
        for s in range(0, count, 2):
            t = jnp.where(low, mf[s, pl.ds(e, 1), :], mf[s + 1, pl.ds(e, 1), :])
            w = jnp.where(low, mf[s, pl.ds(4 + e, 1), :], mf[s + 1, pl.ds(4 + e, 1), :])
            places.append(jnp.where(row_f == t, w, 0.0).astype(BF16))
            for k in range(2):
                blocks.append(load(s + k, pl.ds(pl.multiple_of(64 * e, 64), 64)))
        place = jnp.concatenate(places, axis=1)
        ones = jnp.ones((64 * count, PW), BF16)
        block = jnp.concatenate([jnp.concatenate(blocks, axis=0), ones], axis=1)
        total = jnp.dot(place, block, preferred_element_type=F32)
        d0 = jnp.sum(jnp.where(eye, total[0:PW, PW:], 0.0), axis=0, keepdims=True)
        d1 = jnp.sum(jnp.where(eye, total[PW:, PW:], 0.0), axis=0, keepdims=True)
        den = jnp.where(tile_row == 0, d0, jnp.where(tile_row == 1, d1, 0.0))
        return total[:, 0:PW], den[0:8]

    def dense(ref, lead, total, den):
        high = den.astype(BF16).astype(F32)
        ref[lead + (slice(0, PH), slice(None))] = total.astype(BF16)
        ref[lead + (slice(PH, DENSE), slice(None))] = jnp.concatenate(
            [high, den - high], axis=0
        ).astype(BF16)

    def dense_copy(index, e):
        distance = FAR[index]
        target = jnp.where(
            c == 0,
            patch_of(y, lax.rem(z + distance, SIDE), 0),
            patch_of(lax.rem(y + distance, SIDE), z, 1),
        )
        return pltpu.make_async_remote_copy(
            src_ref=fd.at[index, e], dst_ref=rd.at[index, e],
            send_sem=d_send.at[index, e], recv_sem=d_recv.at[index, e],
            device_id={"patch": target}, device_id_type=MESH,
        )

    def add_far(index):
        @pl.loop(0, 2 * VISITS)
        def _(s):
            pltpu.make_async_copy(rf.at[index, s], rf.at[index, s], f_recv.at[index, s]).wait()

        mf[0 : 2 * VISITS] = rf[index, :, DATA:, :].astype(F32)

        @pl.loop(0, 2)
        def _(e):
            total, den = add_up(2 * VISITS, e, lambda s, rows: rf[index, s, rows, :])
            dense(fd, (index, e), total, den)
            dense_copy(index, e).start()

    groups = PIECES // GROUP

    @pl.loop(0, groups)
    def _(group):
        match_group(group, kind_s, coef_s, plan_s, x, r_ref, g_ref, y_ref, matched_ref)
        fill(group)
        near = group // 2 == 1

        @pl.loop(0, CHUNKS)
        def _(turn):
            @pl.when(near)
            def _():
                send_near(group, turn_part(turn))

            @pl.when(jnp.logical_not(near))
            def _():
                send_far(group, turn_part(turn))

        @pl.when(group == 3)
        def _():
            add_far(0)

    @pl.loop(groups, groups + 2)
    def _(message):
        fill(message)

        @pl.loop(0, CHUNKS)
        def _(turn):
            send_far(message, turn_part(turn))

    @pl.loop(groups + 2, 16)
    def _(message):
        fill(message)
        send_near(message, turn_part(0))

    @pl.loop(1, CHUNKS)
    def _(turn):
        @pl.loop(groups + 2, 16)
        def _(message):
            send_near(message, turn_part(turn))

    add_far(1)
    add_far(2)

    def b_copy(j):
        return pltpu.make_async_remote_copy(
            src_ref=sb.at[j], dst_ref=rbb.at[along],
            send_sem=b_send.at[j], recv_sem=b_recv.at[along],
            device_id={"patch": jnp.where(c == 0, patch_of(j, z, 0), patch_of(y, j, 1))},
            device_id_type=MESH,
        )

    def add_near(turn):
        part = turn_part(turn)

        @pl.loop(0, 2 * len(NEAR))
        def _(s):
            pltpu.make_async_copy(rb.at[s, part], rb.at[s, part], a_recv.at[s, part]).wait()

        mf[...] = rb[:, part, DATA:, :].astype(F32)
        last = turn == CHUNKS - 1
        if last:
            for index in range(len(FAR)):
                for e in range(2):
                    dense_copy(index, e).wait_recv()

        @pl.loop(0, 2)
        def _(e):
            total, den = add_up(2 * len(NEAR), e, lambda s, rows: rb[s, part, rows, :])
            if last:
                for index in range(len(FAR)):
                    total = total + rd[index, e, 0:PH, :].astype(F32)
                    tile = rd[index, e, PH:DENSE, :].astype(F32)
                    den = den + (tile[0:8] + tile[8:16])
            j = part * 2 + e
            dense(sb, (j,), total, den)

            @pl.when(j == along)
            def _():
                pltpu.make_async_copy(sb.at[j], rbb.at[along], b_recv.at[along]).start()

            @pl.when(j != along)
            def _():
                b_copy(j).start()

    for turn in range(CHUNKS):
        add_near(turn)

    num = jnp.zeros((PH, PW), F32)
    den = jnp.zeros((8, PW), F32)
    for i in range(SIDE):
        pltpu.make_async_copy(rbb.at[i], rbb.at[i], b_recv.at[i]).wait()
        num = num + rbb[i, 0:PH, :].astype(F32)
        tile = rbb[i, PH:DENSE, :].astype(F32)
        den = den + (tile[0:8] + tile[8:16])

    edge = jnp.zeros((HALO, PW), F32)
    for at in range(VISITS):
        start = at * STRIP - HALO
        stop = start + SPAN
        if at == 0:
            strip = jnp.concatenate([edge, num[0:stop]], axis=0)
        elif at == VISITS - 1:
            strip = jnp.concatenate([num[start:PH], edge], axis=0)
        else:
            strip = num[start:stop]
        sc[at, 0:SPAN, :] = strip
        sc[at, SPAN:, :] = den

    def c_copy(at):
        return pltpu.make_async_remote_copy(
            src_ref=sc.at[at], dst_ref=rc.at[v], send_sem=c_send.at[at], recv_sem=c_recv.at[v],
            device_id={"visit": at}, device_id_type=MESH,
        )

    @pl.loop(1, VISITS)
    def _(i):
        c_copy(lax.rem(v + i, VISITS)).start()

    pltpu.make_async_copy(sc.at[v], rc.at[v], c_recv.at[v]).start()

    @pl.loop(0, 16)
    def _(message):
        distance = chosen(message // 2, ORDER)
        core = lax.rem(message, 2)
        far = (distance >= 3) & (distance <= 5)

        @pl.loop(0, CHUNKS)
        def _(part):
            here = (core == c) & ((far & (part == v)) | (distance == 0))

            @pl.when(jnp.logical_not(here))
            def _():
                near_copy(message, part, 0, partner).wait_send()

    for index in range(len(FAR)):
        for e in range(2):
            dense_copy(index, e).wait_send()

    @pl.loop(0, SIDE)
    def _(j):
        @pl.when(j != along)
        def _():
            b_copy(j).wait_send()

    total = jnp.zeros((SPAN + 8, PW), F32)
    for i in range(VISITS):
        pltpu.make_async_copy(rc.at[i], rc.at[i], c_recv.at[i]).wait()
        total = total + rc[i]
    sum_ref[...] = total

    @pl.loop(1, VISITS)
    def _(i):
        c_copy(lax.rem(v + i, VISITS)).wait_send()


def filter_kernel(sum_ref, taps_ref, coadd_ref, detection_ref, den_ref, pad_ref):
    v = lax.axis_index("visit")
    half = TD // 2
    pad_ref[...] = jnp.zeros_like(pad_ref)
    pad_ref[0:2, 6 : 6 + TD] = taps_ref[...].astype(F32)
    square = (PW, PW)
    lane, row = iota(square, 1), iota(square, 0)
    taps = jnp.broadcast_to(pad_ref[1:2, :], square)
    cols = pltpu.roll(taps, PW - half - 6, 1, stride=1, stride_axis=0)
    cols = jnp.where(jnp.abs(lane - row) <= half, cols, 0.0).astype(BF16)
    taps = jnp.broadcast_to(pad_ref[0:1, :], (STRIP, PW))
    rows = pltpu.roll(taps, HALO - half - 6, 1, stride=1, stride_axis=0).astype(BF16)
    den_ref[...] = jnp.zeros_like(den_ref)
    for a in range(2):
        column = jnp.broadcast_to(sum_ref[SPAN + a : SPAN + a + 1, :], square).T
        den_ref[HALO + a * PW : HALO + (a + 1) * PW, :] = column
    den = den_ref[pl.ds(pl.multiple_of(v * STRIP, STRIP), SPAN), :]
    coadd = sum_ref[0:SPAN, :] / (1.0 + den)
    coadd_ref[...] = coadd[HALO : HALO + STRIP]
    smoothed = jnp.dot(coadd.astype(BF16), cols, preferred_element_type=F32).astype(BF16)
    smoothed = jnp.concatenate([smoothed, jnp.zeros((PW - SPAN, PW), BF16)], axis=0)
    detection_ref[...] = jnp.dot(rows, smoothed, preferred_element_type=F32)


SMEM = pl.BlockSpec(memory_space=pltpu.SMEM)
VMEM = pl.BlockSpec(memory_space=pltpu.VMEM)


def exchange(pieces, dest, offsets, kernel_index, weights, basis_col, basis_row, coef_table):
    dma = pltpu.SemaphoreType.DMA
    row = (1, PIECES)
    return pl.pallas_call(
        exchange_kernel,
        out_shape=jax.ShapeDtypeStruct((SPAN + 8, PW), F32),
        in_specs=[SMEM] * 2 + [VMEM] * 5 + [pl.BlockSpec(memory_space=pl.ANY)],
        out_specs=VMEM,
        scratch_shapes=[
            pltpu.VMEM((PIECES, PR, PW), BF16),
            pltpu.VMEM((NB * PW, PW), BF16),
            pltpu.VMEM((NB, 4, 8, PW), F32),
            pltpu.VMEM((GROUP * PR, NB * PW), BF16),
            pltpu.VMEM((32, PW), F32),
            pltpu.VMEM((8, PW), F32),
            pltpu.VMEM((8, PW), I32),
            pltpu.SMEM((8, PW), I32),
            pltpu.VMEM((PIECES + 8, PR, PW), BF16),
            pltpu.VMEM((16, CHUNKS, ROWS, PW), BF16),
            pltpu.VMEM((2 * len(NEAR), CHUNKS, ROWS, PW), BF16),
            pltpu.VMEM((len(FAR), 2 * VISITS, ROWS, PW), BF16),
            pltpu.VMEM((2 * len(NEAR), META, PW), F32),
            pltpu.VMEM((len(FAR), 2, DENSE, PW), BF16),
            pltpu.VMEM((len(FAR), 2, DENSE, PW), BF16),
            pltpu.VMEM((SIDE, DENSE, PW), BF16),
            pltpu.VMEM((SIDE, DENSE, PW), BF16),
            pltpu.VMEM((VISITS, SPAN + 8, PW), F32),
            pltpu.VMEM((VISITS, SPAN + 8, PW), F32),
            dma(()),
            dma(()),
            dma((16, CHUNKS)),
            dma((2 * len(NEAR), CHUNKS)),
            dma((len(FAR), 2 * VISITS)),
            dma((len(FAR), 2)),
            dma((len(FAR), 2)),
            dma((SIDE,)),
            dma((SIDE,)),
            dma((VISITS,)),
            dma((VISITS,)),
        ],
        compiler_params=pltpu.CompilerParams(collective_id=0, has_side_effects=True),
        name="exchange",
    )(
        kernel_index, coef_table.T, dest.reshape(row), offsets.reshape(row), weights.reshape(row),
        basis_col, basis_row, pieces,
    )


def finish(sums, det_taps):
    out = jax.ShapeDtypeStruct((STRIP, PW), F32)
    return pl.pallas_call(
        filter_kernel,
        out_shape=(out, out),
        in_specs=[VMEM, VMEM],
        out_specs=(VMEM, VMEM),
        scratch_shapes=[pltpu.VMEM((PH + 2 * HALO, PW), F32), pltpu.VMEM((8, PW), F32)],
        name="finish",
    )(sums, det_taps)


def shards(
    pieces, dest, offsets, kernel_index, weights, basis_col, basis_row, coef_table, det_taps
):
    sums = exchange(
        pieces, dest, offsets, kernel_index, weights, basis_col, basis_row, coef_table
    )
    return finish(sums, det_taps)


def solution(mesh):
    split = P(("patch", "visit"))
    in_specs = (
        P(("patch", "visit"), None, None),
        P(("patch", "visit"), None),
        split,
        split,
        split,
        P(),
        P(),
        P(),
        P(),
    )
    out_specs = (P(("patch", "visit"), None), P(("patch", "visit"), None))
    return jax.shard_map(shards, mesh=mesh, in_specs=in_specs, out_specs=out_specs, check_vma=False)
```

```python
import functools

import jax
import jax.numpy as jnp
from jax import lax
from jax.experimental import pallas as pl
from jax.experimental.pallas import tpu as pltpu
from jax.sharding import PartitionSpec as P

MESH = pl.DeviceIdType.MESH
F32 = jnp.float32
BF16 = jnp.bfloat16
I32 = jnp.int32

PIECES = 96
PR = 32
PW = 128
PH = 256
TAPS = 41
NB = 14
TD = 21
SIDE = 8
VISITS = 4
READY = 1
GROUP = 16
STRIP = PH // VISITS
HALO = 16
SPAN = STRIP + 2 * HALO
SLOTS = 16
META = 16
ROWS = META + SLOTS * PR
LONG = STRIP + 2 * HALO + 8
CHUNKS = 4
CHUNK_DESTS = 8 // CHUNKS
ORDER = (4, 3, 5, 2, 6, 1, 7, 0)


def iota(shape, axis):
    return lax.broadcasted_iota(I32, shape, axis)


def chosen(index, values):
    result = jnp.full_like(index, values[-1])
    for at, value in enumerate(values[:-1]):
        result = jnp.where(index == at, value, result)
    return result


def tables(col_ref, row_ref, pad_ref, g_ref, r_ref):
    half = TAPS // 2
    pad_ref[...] = jnp.zeros_like(pad_ref)
    pad_ref[0:NB, 4 : 4 + TAPS] = col_ref[...].astype(F32)
    pad_ref[16 : 16 + NB, 4 : 4 + TAPS] = row_ref[...].astype(F32)
    band = jnp.abs(iota((PW, PW), 1) - iota((PW, PW), 0)) <= half
    row_lane = iota((PR, PW), 1)
    row_band = (jnp.abs(row_lane - iota((PR, PW), 0)) <= half) & (row_lane < PR)
    for b in range(NB):
        taps = jnp.broadcast_to(pad_ref[b : b + 1, :], (PW, PW))
        g = pltpu.roll(taps, PW - half - 4, 1, stride=1, stride_axis=0)
        g_ref[b * PW : (b + 1) * PW, :] = jnp.where(band, g, 0.0).astype(BF16)
        taps = jnp.broadcast_to(pad_ref[16 + b : 17 + b, :], (PR, PW))
        r = pltpu.roll(taps, PW - half - 4, 1, stride=1, stride_axis=0)
        r = jnp.where(row_band, r, 0.0)
        r = r + pltpu.roll(r, 32, 1) + pltpu.roll(r, 64, 1) + pltpu.roll(r, 96, 1)
        r_ref[b] = r.reshape(4, 8, PW)


def plan(y, z, c, dest_ref, off_ref, weight_ref, plan_ref, padf_ref, stage_ref):
    plan_ref[...] = jnp.full_like(plan_ref, -1)
    plan_ref[0:1, 0:PIECES] = dest_ref[...]
    padf_ref[...] = jnp.zeros_like(padf_ref)
    padf_ref[0:1, 0:PIECES] = off_ref[...].astype(F32)
    padf_ref[1:2, 0:PIECES] = weight_ref[...].astype(F32)
    square = (PW, PW)
    lane, row = iota(square, 1), iota(square, 0)
    d = jnp.broadcast_to(plan_ref[0:1, :], square)
    d_t = d.T
    earlier = jnp.sum(jnp.where((d == d_t) & (row < lane), 1, 0), axis=0, keepdims=True)
    d1 = plan_ref[0:1, :]
    y_to, z_to, c_to = d1 >> 4, (d1 >> 1) & 7, d1 & 1
    distance = jnp.where(c_to == 0, z_to - z, y_to - y)
    distance = jnp.where(c_to == c, distance, -distance) & 7
    inner = jnp.where(c_to == 0, y_to, z_to)
    turn = chosen(distance, tuple(ORDER.index(o) for o in range(SIDE)))
    position = ((turn * 2 + c_to) * 8 + inner) * 2 + earlier
    lane1 = iota((1, PW), 1)
    position = jnp.where(lane1 < PIECES, position, 1024 + lane1)
    pos = jnp.broadcast_to(position, square)
    pos_t = pos.T
    rank = jnp.sum(jnp.where(pos_t < pos, 1, 0), axis=0, keepdims=True)
    rank_t = jnp.broadcast_to(rank, square).T
    order = jnp.sum(jnp.where(rank_t == lane, row, 0), axis=0, keepdims=True)
    plan_ref[0:1, :] = order
    for a in range(2):
        plan_ref[1 + a : 2 + a, :] = PIECES + jnp.sum(
            jnp.where(pos_t == lane + a * PW, rank_t - PIECES, 0), axis=0, keepdims=True
        )
    which = (lane // PR) & 1
    hot = jnp.concatenate(
        [jnp.where(pos == 2 * row + k, 1.0, 0.0).astype(BF16) for k in range(2)], axis=1
    )
    found = []
    for at in range(2):
        value = jnp.broadcast_to(padf_ref[at : at + 1, :], square).T
        value = jnp.concatenate(
            [jnp.where(which == k, value, 0.0).astype(BF16) for k in range(2)], axis=0
        )
        found.append(jnp.dot(hot, value, preferred_element_type=F32))
    target = found[0] + (lane & (PR - 1)).astype(F32)
    stage_ref[:, 0:META, :] = jnp.concatenate(
        [target.reshape(16, 8, PW), found[1].reshape(16, 8, PW)], axis=1
    ).astype(BF16)


def match_group(group, kind_s, coef_s, plan_s, x, r_ref, g_ref, y_ref, matched_ref):
    first = group * GROUP
    lane8 = iota((8, PW), 1)
    zeros = jnp.zeros((PR, PW), BF16)
    for quad in range(GROUP // 4):
        pieces = [plan_s[0, first + quad * 4 + j] for j in range(4)]
        kinds = [kind_s[n] for n in pieces]
        parts = []
        for b in range(NB):
            factor = jnp.where(
                lane8 < 64,
                jnp.where(lane8 < 32, coef_s[b, kinds[0]], coef_s[b, kinds[1]]),
                jnp.where(lane8 < 96, coef_s[b, kinds[2]], coef_s[b, kinds[3]]),
            )
            parts.append((r_ref[b] * factor[None]).reshape(PR, PW))
        row_kernel = jnp.concatenate(parts, axis=0).astype(BF16)
        images = [x[n] for n in pieces]
        for pair in range(2):
            rows = []
            for j in range(4):
                left = images[j] if j == 2 * pair else zeros
                right = images[j] if j == 2 * pair + 1 else zeros
                rows.append(jnp.concatenate([left, right], axis=1))
            both = jnp.concatenate(rows, axis=0)
            y = jnp.dot(row_kernel, both, preferred_element_type=F32).astype(BF16)
            for j in range(2):
                at = (quad * 4 + pair * 2 + j) * PR
                for b in range(NB):
                    y_ref[at : at + PR, b * PW : (b + 1) * PW] = y[
                        b * PR : (b + 1) * PR, j * PW : (j + 1) * PW
                    ]
    matched = jnp.dot(y_ref[...], g_ref[...], preferred_element_type=F32).astype(BF16)
    matched_ref[pl.ds(first, GROUP)] = matched.reshape(GROUP, PR, PW)


def exchange_kernel(
    kind_in, coef_in, dest_in, off_in, weight_in, col_in, row_in, pieces_ref,
    sum_ref,
    kind_s, coef_s, dest_ref, off_ref, weight_ref, col_ref, row_ref, x, g_ref, r_ref, y_ref, pad_ref, padf_ref, plan_ref, plan_s, matched_ref, stage_ref,
    rb, mf, sb, rbb, sc, rc,
    in_sem, x_sem, plan_sem, a_send, a_recv, b_send, b_recv, c_send, c_recv,
):
    p = lax.axis_index("patch")
    v = lax.axis_index("visit")
    c = lax.rem(p, 2)
    z = lax.rem(p // 2, SIDE)
    y = p // (2 * SIDE)
    along = jnp.where(c == 0, y, z)

    def patch_of(y_at, z_at, c_at):
        return (y_at * SIDE + z_at) * 2 + c_at

    small = [
        pltpu.make_async_copy(source, target, in_sem.at[at])
        for at, (source, target) in enumerate(
            (
                (dest_in, dest_ref), (off_in, off_ref), (weight_in, weight_ref),
                (col_in, col_ref), (row_in, row_ref), (kind_in, kind_s), (coef_in, coef_s),
            )
        )
    ]
    for copy in small:
        copy.start()
    x_copy = pltpu.make_async_copy(pieces_ref, x, x_sem)
    x_copy.start()

    barrier = pltpu.get_barrier_semaphore()

    def greet(target):
        pl.semaphore_signal(barrier, inc=1, device_id={"patch": target}, device_id_type=MESH)

    @pl.loop(1, SIDE)
    def _(i):
        for core in range(2):
            greet(patch_of(y, lax.rem(z + i, SIDE), core))
            greet(patch_of(lax.rem(y + i, SIDE), z, core))

    greet(patch_of(y, z, 1 - c))

    @pl.loop(1, VISITS)
    def _(i):
        pl.semaphore_signal(
            barrier, inc=1, device_id={"visit": lax.rem(v + i, VISITS)}, device_id_type=MESH
        )

    for copy in small:
        copy.wait()
    plan(y, z, c, dest_ref, off_ref, weight_ref, plan_ref, padf_ref, stage_ref)
    plan_copy = pltpu.make_async_copy(plan_ref, plan_s, plan_sem)
    plan_copy.start()
    tables(col_ref, row_ref, pad_ref, g_ref, r_ref)
    matched_ref[PIECES:, :, :] = jnp.zeros((8, PR, PW), BF16)
    plan_copy.wait()
    x_copy.wait()

    def part_of(ref, at, part):
        if part == 0:
            return ref.at[at, pl.ds(0, META + CHUNK_DESTS * 64)]
        return ref.at[at, pl.ds(META + part * CHUNK_DESTS * 64, CHUNK_DESTS * 64)]

    def a_copy(message, part, slot, target):
        return pltpu.make_async_remote_copy(
            src_ref=part_of(stage_ref, message, part), dst_ref=part_of(rb, slot, part),
            send_sem=a_send.at[part, message], recv_sem=a_recv.at[part, slot],
            device_id={"patch": target}, device_id_type=MESH,
        )

    z_slot = z * 2 + c
    y_slot = y * 2 + c
    partner = patch_of(y, z, 1 - c)
    here = 2 * (SIDE - 1) + c

    def fill(message):
        for s in range(SLOTS):
            r = plan_s[1 + message // 8, (message % 8) * SLOTS + s]
            stage_ref[message, META + s * PR : META + (s + 1) * PR, :] = matched_ref[r]

    def send(message, part):
        even = lax.rem(message, 2) == 0
        distance = chosen(message // 2, ORDER)
        distance = jnp.where(lax.rem(message, 2) == c, distance, lax.rem(SIDE - distance, SIDE))
        target = jnp.where(
            even,
            patch_of(y, lax.rem(z + distance, SIDE), 0),
            patch_of(lax.rem(y + distance, SIDE), z, 1),
        )
        slot = jnp.where(even, z_slot, y_slot)

        @pl.when(message != here)
        def _():
            a_copy(message, part, slot, target).start()

        @pl.when(message == here)
        def _():
            pltpu.make_async_copy(
                part_of(stage_ref, message, part), part_of(rb, slot, part), a_recv.at[part, slot]
            ).start()

    def send_fixed(message, part):
        core = message % 2
        distance = ORDER[message // 2]
        step = jnp.where(c == core, distance, (SIDE - distance) % SIDE)
        if core == 0:
            target, slot = patch_of(y, lax.rem(z + step, SIDE), 0), z_slot
        else:
            target, slot = patch_of(lax.rem(y + step, SIDE), z, 1), y_slot
        if distance:
            a_copy(message, part, slot, target).start()
        else:

            @pl.when(c != core)
            def _():
                a_copy(message, part, slot, target).start()

            @pl.when(c == core)
            def _():
                pltpu.make_async_copy(
                    part_of(stage_ref, message, part), part_of(rb, slot, part),
                    a_recv.at[part, slot],
                ).start()

    groups = PIECES // GROUP

    @pl.loop(0, groups)
    def _(group):
        match_group(group, kind_s, coef_s, plan_s, x, r_ref, g_ref, y_ref, matched_ref)
        fill(group)

        @pl.when(group == READY)
        def _():
            pl.semaphore_wait(barrier, 4 * (SIDE - 1) + 1 + VISITS - 1)

            @pl.loop(0, READY)
            def _(message):
                for part in range(CHUNKS):
                    send(message, part)

        @pl.when(group >= READY)
        def _():
            for part in range(CHUNKS):
                send(group, part)

    for part in range(CHUNKS):
        for message in range(groups, 16):
            if part == 0:
                fill(message)
            send_fixed(message, part)

    row_f = iota((PH, PW), 0).astype(F32)
    low = iota((1, PW), 1) < 64
    eye = iota((PW, PW), 0) == iota((PW, PW), 1)
    tile_row = iota((8, PW), 0)
    ones = jnp.ones((4 * 64, PW), BF16)
    edge = jnp.zeros((HALO, PW), F32)

    def split(den):
        high = den.astype(BF16).astype(F32)
        return jnp.where(tile_row < 4, high, pltpu.roll(den - high, 4, 0))

    def joined(tile):
        return tile + pltpu.roll(tile, 4, 0)

    def b_copy(part, at):
        return pltpu.make_async_remote_copy(
            src_ref=sb.at[part, at], dst_ref=rbb.at[v, part],
            send_sem=b_send.at[part, at], recv_sem=b_recv.at[part, v],
            device_id={"visit": at}, device_id_type=MESH,
        )

    def add_up(part):
        @pl.loop(0, 16)
        def _(s):
            a_copy(s, part, s, partner).wait_recv()

        if part == 0:
            mf[...] = rb[:, 0:META, :].astype(F32)

        @pl.loop(0, CHUNK_DESTS)
        def _(e):
            j = part * CHUNK_DESTS + e
            total = jnp.zeros((PH, 2 * PW), F32)
            for four in range(4):
                places = []
                blocks = []
                for pair in range(2):
                    s = four * 4 + pair * 2
                    t = jnp.where(low, mf[s, pl.ds(j, 1), :], mf[s + 1, pl.ds(j, 1), :])
                    w = jnp.where(low, mf[s, pl.ds(8 + j, 1), :], mf[s + 1, pl.ds(8 + j, 1), :])
                    places.append(jnp.where(row_f == t, w, 0.0).astype(BF16))
                    for k in range(2):
                        blocks.append(rb[s + k, pl.ds(pl.multiple_of(META + 64 * j, 16), 64), :])
                place = jnp.concatenate(places, axis=1)
                block = jnp.concatenate([jnp.concatenate(blocks, axis=0), ones], axis=1)
                total = total + jnp.dot(place, block, preferred_element_type=F32)
            d0 = jnp.sum(jnp.where(eye, total[0:PW, PW:], 0.0), axis=0, keepdims=True)
            d1 = jnp.sum(jnp.where(eye, total[PW:, PW:], 0.0), axis=0, keepdims=True)
            den = jnp.where(tile_row == 0, d0, jnp.where(tile_row == 1, d1, 0.0))
            tile = split(den).astype(BF16)
            for at in range(VISITS):
                start = at * STRIP - HALO
                stop = start + SPAN
                if at == 0:
                    strip = jnp.concatenate([edge, total[0:stop, 0:PW]], axis=0)
                elif at == VISITS - 1:
                    strip = jnp.concatenate([total[start:PH, 0:PW], edge], axis=0)
                else:
                    strip = total[start:stop, 0:PW]
                sb[part, at, e, 0:SPAN, :] = strip.astype(BF16)
                sb[part, at, e, SPAN:, :] = tile

        @pl.loop(1, VISITS)
        def _(i):
            b_copy(part, lax.rem(v + i, VISITS)).start()

        pltpu.make_async_copy(sb.at[part, v], rbb.at[v, part], b_recv.at[part, v]).start()

    def c_copy(j):
        return pltpu.make_async_remote_copy(
            src_ref=sc.at[j], dst_ref=rc.at[along],
            send_sem=c_send.at[j], recv_sem=c_recv.at[along],
            device_id={"patch": jnp.where(c == 0, patch_of(j, z, 0), patch_of(y, j, 1))},
            device_id_type=MESH,
        )

    def collect(part):
        for at in range(VISITS):
            pltpu.make_async_copy(rbb.at[at, part], rbb.at[at, part], b_recv.at[part, at]).wait()

        for e in range(CHUNK_DESTS):
            j = part * CHUNK_DESTS + e
            total = rbb[0, part, e].astype(F32)
            for at in range(1, VISITS):
                total = total + rbb[at, part, e].astype(F32)
            sc[j, 0:SPAN, :] = total[0:SPAN].astype(BF16)
            sc[j, SPAN:, :] = split(joined(total[SPAN:])).astype(BF16)

            @pl.when(j == along)
            def _():
                pltpu.make_async_copy(sc.at[j], rc.at[along], c_recv.at[along]).start()

            @pl.when(j != along)
            def _():
                c_copy(j).start()

    add_up(0)
    for part in range(1, CHUNKS):
        add_up(part)
        collect(part - 1)
    collect(CHUNKS - 1)

    for part in range(CHUNKS):

        @pl.loop(0, 16)
        def _(message):
            @pl.when(message != here)
            def _():
                a_copy(message, part, z_slot, partner).wait_send()

        @pl.loop(1, VISITS)
        def _(i):
            b_copy(part, lax.rem(v + i, VISITS)).wait_send()

    total = jnp.zeros((LONG, PW), F32)
    for i in range(SIDE):
        pltpu.make_async_copy(rc.at[i], rc.at[i], c_recv.at[i]).wait()
        total = total + rc[i].astype(F32)
    sum_ref[0:SPAN, :] = total[0:SPAN]
    sum_ref[SPAN:, :] = joined(total[SPAN:])

    @pl.loop(0, SIDE)
    def _(j):
        @pl.when(j != along)
        def _():
            c_copy(j).wait_send()


def filter_kernel(sum_ref, taps_ref, coadd_ref, detection_ref, den_ref, pad_ref):
    v = lax.axis_index("visit")
    half = TD // 2
    pad_ref[...] = jnp.zeros_like(pad_ref)
    pad_ref[0:2, 6 : 6 + TD] = taps_ref[...].astype(F32)
    square = (PW, PW)
    lane, row = iota(square, 1), iota(square, 0)
    taps = jnp.broadcast_to(pad_ref[1:2, :], square)
    cols = pltpu.roll(taps, PW - half - 6, 1, stride=1, stride_axis=0)
    cols = jnp.where(jnp.abs(lane - row) <= half, cols, 0.0).astype(BF16)
    taps = jnp.broadcast_to(pad_ref[0:1, :], (STRIP, PW))
    rows = pltpu.roll(taps, HALO - half - 6, 1, stride=1, stride_axis=0).astype(BF16)
    den_ref[...] = jnp.zeros_like(den_ref)
    for a in range(2):
        column = jnp.broadcast_to(sum_ref[SPAN + a : SPAN + a + 1, :], square).T
        den_ref[HALO + a * PW : HALO + (a + 1) * PW, :] = column
    den = den_ref[pl.ds(pl.multiple_of(v * STRIP, STRIP), SPAN), :]
    coadd = sum_ref[0:SPAN, :] / (1.0 + den)
    coadd_ref[...] = coadd[HALO : HALO + STRIP]
    smoothed = jnp.dot(coadd.astype(BF16), cols, preferred_element_type=F32).astype(BF16)
    smoothed = jnp.concatenate([smoothed, jnp.zeros((PW - SPAN, PW), BF16)], axis=0)
    detection_ref[...] = jnp.dot(rows, smoothed, preferred_element_type=F32)


VMEM = pl.BlockSpec(memory_space=pltpu.VMEM)


def exchange(pieces, dest, offsets, kernel_index, weights, basis_col, basis_row, coef_table):
    dma = pltpu.SemaphoreType.DMA
    row = (1, PIECES)
    return pl.pallas_call(
        exchange_kernel,
        out_shape=pltpu.VMEM((LONG, PW), F32),
        in_specs=[pl.BlockSpec(memory_space=pl.ANY)] * 8,
        out_specs=VMEM,
        scratch_shapes=[
            pltpu.SMEM((PIECES,), I32),
            pltpu.SMEM(coef_table.shape[::-1], F32),
            pltpu.VMEM(row, I32),
            pltpu.VMEM(row, I32),
            pltpu.VMEM(row, BF16),
            pltpu.VMEM(basis_col.shape, BF16),
            pltpu.VMEM(basis_row.shape, BF16),
            pltpu.VMEM((PIECES, PR, PW), BF16),
            pltpu.VMEM((NB * PW, PW), BF16),
            pltpu.VMEM((NB, 4, 8, PW), F32),
            pltpu.VMEM((GROUP * PR, NB * PW), BF16),
            pltpu.VMEM((32, PW), F32),
            pltpu.VMEM((8, PW), F32),
            pltpu.VMEM((8, PW), I32),
            pltpu.SMEM((8, PW), I32),
            pltpu.VMEM((PIECES + 8, PR, PW), BF16),
            pltpu.VMEM((16, ROWS, PW), BF16),
            pltpu.VMEM((16, ROWS, PW), BF16),
            pltpu.VMEM((16, META, PW), F32),
            pltpu.VMEM((CHUNKS, VISITS, CHUNK_DESTS, LONG, PW), BF16),
            pltpu.VMEM((VISITS, CHUNKS, CHUNK_DESTS, LONG, PW), BF16),
            pltpu.VMEM((SIDE, LONG, PW), BF16),
            pltpu.VMEM((SIDE, LONG, PW), BF16),
            dma((7,)),
            dma(()),
            dma(()),
            dma((CHUNKS, 16)),
            dma((CHUNKS, 16)),
            dma((CHUNKS, VISITS)),
            dma((CHUNKS, VISITS)),
            dma((SIDE,)),
            dma((SIDE,)),
        ],
        compiler_params=pltpu.CompilerParams(collective_id=0, has_side_effects=True),
        name="exchange",
    )(
        kernel_index, coef_table.T, dest.reshape(row), offsets.reshape(row), weights.reshape(row),
        basis_col, basis_row, pieces,
    )


def finish(sums, det_taps):
    out = jax.ShapeDtypeStruct((STRIP, PW), F32)
    return pl.pallas_call(
        filter_kernel,
        out_shape=(out, out),
        in_specs=[VMEM, VMEM],
        out_specs=(VMEM, VMEM),
        scratch_shapes=[pltpu.VMEM((PH + 2 * HALO, PW), F32), pltpu.VMEM((8, PW), F32)],
        name="finish",
    )(pltpu.with_memory_space_constraint(sums, pltpu.VMEM), det_taps)


def shards(
    pieces, dest, offsets, kernel_index, weights, basis_col, basis_row, coef_table, det_taps
):
    sums = exchange(
        pieces, dest, offsets, kernel_index, weights, basis_col, basis_row, coef_table
    )
    return finish(sums, det_taps)


def solution(mesh):
    split = P(("patch", "visit"))
    in_specs = (
        P(("patch", "visit"), None, None),
        P(("patch", "visit"), None),
        split,
        split,
        split,
        P(),
        P(),
        P(),
        P(),
    )
    out_specs = (P(("patch", "visit"), None), P(("patch", "visit"), None))
    return jax.shard_map(shards, mesh=mesh, in_specs=in_specs, out_specs=out_specs, check_vma=False)
```

```python
import functools

import jax
import jax.numpy as jnp
from jax import lax
from jax.experimental import pallas as pl
from jax.experimental.pallas import tpu as pltpu
from jax.sharding import PartitionSpec as P

MESH = pl.DeviceIdType.MESH
F32 = jnp.float32
BF16 = jnp.bfloat16
I32 = jnp.int32

PIECES = 96
PR = 32
PW = 128
PH = 256
TAPS = 41
NB = 14
TD = 21
SIDE = 8
VISITS = 4
READY = 1
GROUP = 16
STRIP = PH // VISITS
HALO = 16
SPAN = STRIP + 2 * HALO
SLOTS = 16
META = 16
ROWS = META + SLOTS * PR
LONG = STRIP + 2 * HALO + 8
PARTS = (3, 2, 2, 1)
CHUNKS = len(PARTS)
FIRST = tuple(sum(PARTS[:part]) for part in range(CHUNKS))
EARLY = 2
ORDER = (4, 3, 5, 2, 6, 1, 7, 0)


def iota(shape, axis):
    return lax.broadcasted_iota(I32, shape, axis)


def chosen(index, values):
    result = jnp.full_like(index, values[-1])
    for at, value in enumerate(values[:-1]):
        result = jnp.where(index == at, value, result)
    return result


def tables(col_ref, row_ref, pad_ref, g_ref, r_ref):
    half = TAPS // 2
    pad_ref[...] = jnp.zeros_like(pad_ref)
    pad_ref[0:NB, 4 : 4 + TAPS] = col_ref[...].astype(F32)
    pad_ref[16 : 16 + NB, 4 : 4 + TAPS] = row_ref[...].astype(F32)
    band = jnp.abs(iota((PW, PW), 1) - iota((PW, PW), 0)) <= half
    row_lane = iota((PR, PW), 1)
    row_band = (jnp.abs(row_lane - iota((PR, PW), 0)) <= half) & (row_lane < PR)
    for b in range(NB):
        taps = jnp.broadcast_to(pad_ref[b : b + 1, :], (PW, PW))
        g = pltpu.roll(taps, PW - half - 4, 1, stride=1, stride_axis=0)
        g_ref[b * PW : (b + 1) * PW, :] = jnp.where(band, g, 0.0).astype(BF16)
        taps = jnp.broadcast_to(pad_ref[16 + b : 17 + b, :], (PR, PW))
        r = pltpu.roll(taps, PW - half - 4, 1, stride=1, stride_axis=0)
        r = jnp.where(row_band, r, 0.0)
        r = r + pltpu.roll(r, 32, 1) + pltpu.roll(r, 64, 1) + pltpu.roll(r, 96, 1)
        r_ref[b] = r.reshape(4, 8, PW)


def plan(y, z, c, dest_ref, off_ref, weight_ref, plan_ref, padf_ref, stage_ref):
    plan_ref[...] = jnp.full_like(plan_ref, -1)
    plan_ref[0:1, 0:PIECES] = dest_ref[...]
    padf_ref[...] = jnp.zeros_like(padf_ref)
    padf_ref[0:1, 0:PIECES] = off_ref[...].astype(F32)
    padf_ref[1:2, 0:PIECES] = weight_ref[...].astype(F32)
    square = (PW, PW)
    lane, row = iota(square, 1), iota(square, 0)
    d = jnp.broadcast_to(plan_ref[0:1, :], square)
    d_t = d.T
    earlier = jnp.sum(jnp.where((d == d_t) & (row < lane), 1, 0), axis=0, keepdims=True)
    d1 = plan_ref[0:1, :]
    y_to, z_to, c_to = d1 >> 4, (d1 >> 1) & 7, d1 & 1
    distance = jnp.where(c_to == 0, z_to - z, y_to - y)
    distance = jnp.where(c_to == c, distance, -distance) & 7
    inner = jnp.where(c_to == 0, y_to, z_to)
    turn = chosen(distance, tuple(ORDER.index(o) for o in range(SIDE)))
    position = ((turn * 2 + c_to) * 8 + inner) * 2 + earlier
    lane1 = iota((1, PW), 1)
    position = jnp.where(lane1 < PIECES, position, 1024 + lane1)
    pos = jnp.broadcast_to(position, square)
    pos_t = pos.T
    rank = jnp.sum(jnp.where(pos_t < pos, 1, 0), axis=0, keepdims=True)
    rank_t = jnp.broadcast_to(rank, square).T
    order = jnp.sum(jnp.where(rank_t == lane, row, 0), axis=0, keepdims=True)
    plan_ref[0:1, :] = order
    for a in range(2):
        plan_ref[1 + a : 2 + a, :] = PIECES + jnp.sum(
            jnp.where(pos_t == lane + a * PW, rank_t - PIECES, 0), axis=0, keepdims=True
        )
    which = (lane // PR) & 1
    hot = jnp.concatenate(
        [jnp.where(pos == 2 * row + k, 1.0, 0.0).astype(BF16) for k in range(2)], axis=1
    )
    found = []
    for at in range(2):
        value = jnp.broadcast_to(padf_ref[at : at + 1, :], square).T
        value = jnp.concatenate(
            [jnp.where(which == k, value, 0.0).astype(BF16) for k in range(2)], axis=0
        )
        found.append(jnp.dot(hot, value, preferred_element_type=F32))
    target = found[0] + (lane & (PR - 1)).astype(F32)
    stage_ref[:, 0:META, :] = jnp.concatenate(
        [target.reshape(16, 8, PW), found[1].reshape(16, 8, PW)], axis=1
    ).astype(BF16)


def match_group(group, kind_s, coef_s, plan_s, x, r_ref, g_ref, y_ref, matched_ref):
    first = group * GROUP
    lane8 = iota((8, PW), 1)
    zeros = jnp.zeros((PR, PW), BF16)
    for quad in range(GROUP // 4):
        pieces = [plan_s[0, first + quad * 4 + j] for j in range(4)]
        kinds = [kind_s[n] for n in pieces]
        parts = []
        for b in range(NB):
            factor = jnp.where(
                lane8 < 64,
                jnp.where(lane8 < 32, coef_s[b, kinds[0]], coef_s[b, kinds[1]]),
                jnp.where(lane8 < 96, coef_s[b, kinds[2]], coef_s[b, kinds[3]]),
            )
            parts.append((r_ref[b] * factor[None]).reshape(PR, PW))
        row_kernel = jnp.concatenate(parts, axis=0).astype(BF16)
        images = [x[n] for n in pieces]
        for pair in range(2):
            rows = []
            for j in range(4):
                left = images[j] if j == 2 * pair else zeros
                right = images[j] if j == 2 * pair + 1 else zeros
                rows.append(jnp.concatenate([left, right], axis=1))
            both = jnp.concatenate(rows, axis=0)
            y = jnp.dot(row_kernel, both, preferred_element_type=F32).astype(BF16)
            for j in range(2):
                at = (quad * 4 + pair * 2 + j) * PR
                for b in range(NB):
                    y_ref[at : at + PR, b * PW : (b + 1) * PW] = y[
                        b * PR : (b + 1) * PR, j * PW : (j + 1) * PW
                    ]
    matched = jnp.dot(y_ref[...], g_ref[...], preferred_element_type=F32).astype(BF16)
    matched_ref[pl.ds(first, GROUP)] = matched.reshape(GROUP, PR, PW)


def exchange_kernel(
    kind_in, coef_in, dest_in, off_in, weight_in, col_in, row_in, pieces_ref,
    sum_ref,
    kind_s, coef_s, dest_ref, off_ref, weight_ref, col_ref, row_ref, x, g_ref, r_ref, y_ref, pad_ref, padf_ref, plan_ref, plan_s, matched_ref, stage_ref,
    rb, mf, sb, rbb, sc, rc,
    in_sem, x_sem, plan_sem, a_send, a_recv, b_send, b_recv, c_send, c_recv,
):
    p = lax.axis_index("patch")
    v = lax.axis_index("visit")
    c = lax.rem(p, 2)
    z = lax.rem(p // 2, SIDE)
    y = p // (2 * SIDE)
    along = jnp.where(c == 0, y, z)

    def patch_of(y_at, z_at, c_at):
        return (y_at * SIDE + z_at) * 2 + c_at

    small = [
        pltpu.make_async_copy(source, target, in_sem.at[at])
        for at, (source, target) in enumerate(
            (
                (dest_in, dest_ref), (off_in, off_ref), (weight_in, weight_ref),
                (col_in, col_ref), (row_in, row_ref), (kind_in, kind_s), (coef_in, coef_s),
            )
        )
    ]
    for copy in small:
        copy.start()
    x_copy = pltpu.make_async_copy(pieces_ref, x, x_sem)
    x_copy.start()

    barrier = pltpu.get_barrier_semaphore()

    def greet(target):
        pl.semaphore_signal(barrier, inc=1, device_id={"patch": target}, device_id_type=MESH)

    @pl.loop(1, SIDE)
    def _(i):
        for core in range(2):
            greet(patch_of(y, lax.rem(z + i, SIDE), core))
            greet(patch_of(lax.rem(y + i, SIDE), z, core))

    greet(patch_of(y, z, 1 - c))

    @pl.loop(1, VISITS)
    def _(i):
        pl.semaphore_signal(
            barrier, inc=1, device_id={"visit": lax.rem(v + i, VISITS)}, device_id_type=MESH
        )

    for copy in small:
        copy.wait()
    plan(y, z, c, dest_ref, off_ref, weight_ref, plan_ref, padf_ref, stage_ref)
    plan_copy = pltpu.make_async_copy(plan_ref, plan_s, plan_sem)
    plan_copy.start()
    tables(col_ref, row_ref, pad_ref, g_ref, r_ref)
    matched_ref[PIECES:, :, :] = jnp.zeros((8, PR, PW), BF16)
    plan_copy.wait()
    x_copy.wait()

    def part_of(ref, at, part):
        if part == 0:
            return ref.at[at, pl.ds(0, META + PARTS[0] * 64)]
        return ref.at[at, pl.ds(META + FIRST[part] * 64, PARTS[part] * 64)]

    def a_copy(message, part, slot, target):
        return pltpu.make_async_remote_copy(
            src_ref=part_of(stage_ref, message, part), dst_ref=part_of(rb, slot, part),
            send_sem=a_send.at[part, message], recv_sem=a_recv.at[part, slot],
            device_id={"patch": target}, device_id_type=MESH,
        )

    z_slot = z * 2 + c
    y_slot = y * 2 + c
    partner = patch_of(y, z, 1 - c)
    here = 2 * (SIDE - 1) + c

    def fill(message):
        for s in range(SLOTS):
            r = plan_s[1 + message // 8, (message % 8) * SLOTS + s]
            stage_ref[message, META + s * PR : META + (s + 1) * PR, :] = matched_ref[r]

    def send(message, part):
        even = lax.rem(message, 2) == 0
        distance = chosen(message // 2, ORDER)
        distance = jnp.where(lax.rem(message, 2) == c, distance, lax.rem(SIDE - distance, SIDE))
        target = jnp.where(
            even,
            patch_of(y, lax.rem(z + distance, SIDE), 0),
            patch_of(lax.rem(y + distance, SIDE), z, 1),
        )
        slot = jnp.where(even, z_slot, y_slot)

        @pl.when(message != here)
        def _():
            a_copy(message, part, slot, target).start()

        @pl.when(message == here)
        def _():
            pltpu.make_async_copy(
                part_of(stage_ref, message, part), part_of(rb, slot, part), a_recv.at[part, slot]
            ).start()

    def send_fixed(message, part):
        core = message % 2
        distance = ORDER[message // 2]
        step = jnp.where(c == core, distance, (SIDE - distance) % SIDE)
        if core == 0:
            target, slot = patch_of(y, lax.rem(z + step, SIDE), 0), z_slot
        else:
            target, slot = patch_of(lax.rem(y + step, SIDE), z, 1), y_slot
        if distance:
            a_copy(message, part, slot, target).start()
        else:

            @pl.when(c != core)
            def _():
                a_copy(message, part, slot, target).start()

            @pl.when(c == core)
            def _():
                pltpu.make_async_copy(
                    part_of(stage_ref, message, part), part_of(rb, slot, part),
                    a_recv.at[part, slot],
                ).start()

    groups = PIECES // GROUP

    @pl.loop(0, groups)
    def _(group):
        match_group(group, kind_s, coef_s, plan_s, x, r_ref, g_ref, y_ref, matched_ref)
        fill(group)

        @pl.when(group == READY)
        def _():
            pl.semaphore_wait(barrier, 4 * (SIDE - 1) + 1 + VISITS - 1)

            @pl.loop(0, READY)
            def _(message):
                for part in range(EARLY):
                    send(message, part)

        @pl.when(group >= READY)
        def _():
            for part in range(EARLY):
                send(group, part)

    for part in range(CHUNKS):
        for message in range(groups if part < EARLY else 0, 16):
            if part == 0:
                fill(message)
            send_fixed(message, part)

    row_f = iota((PH, PW), 0).astype(F32)
    low = iota((1, PW), 1) < 64
    eye = iota((PW, PW), 0) == iota((PW, PW), 1)
    tile_row = iota((8, PW), 0)
    ones = jnp.ones((4 * 64, PW), BF16)
    edge = jnp.zeros((HALO, PW), F32)

    def split(den):
        high = den.astype(BF16).astype(F32)
        return jnp.where(tile_row < 4, high, pltpu.roll(den - high, 4, 0))

    def joined(tile):
        return tile + pltpu.roll(tile, 4, 0)

    def strips_of(ref, at, part):
        return ref.at[at, pl.ds(FIRST[part], PARTS[part])]

    def b_copy(part, at):
        return pltpu.make_async_remote_copy(
            src_ref=strips_of(sb, at, part), dst_ref=strips_of(rbb, v, part),
            send_sem=b_send.at[part, at], recv_sem=b_recv.at[part, v],
            device_id={"visit": at}, device_id_type=MESH,
        )

    def add_up(part):
        @pl.loop(0, 16)
        def _(s):
            a_copy(s, part, s, partner).wait_recv()

        if part == 0:
            mf[...] = rb[:, 0:META, :].astype(F32)

        @pl.loop(FIRST[part], FIRST[part] + PARTS[part])
        def _(j):
            total = jnp.zeros((PH, 2 * PW), F32)
            for four in range(4):
                places = []
                blocks = []
                for pair in range(2):
                    s = four * 4 + pair * 2
                    t = jnp.where(low, mf[s, pl.ds(j, 1), :], mf[s + 1, pl.ds(j, 1), :])
                    w = jnp.where(low, mf[s, pl.ds(8 + j, 1), :], mf[s + 1, pl.ds(8 + j, 1), :])
                    places.append(jnp.where(row_f == t, w, 0.0).astype(BF16))
                    for k in range(2):
                        blocks.append(rb[s + k, pl.ds(pl.multiple_of(META + 64 * j, 16), 64), :])
                place = jnp.concatenate(places, axis=1)
                block = jnp.concatenate([jnp.concatenate(blocks, axis=0), ones], axis=1)
                total = total + jnp.dot(place, block, preferred_element_type=F32)
            d0 = jnp.sum(jnp.where(eye, total[0:PW, PW:], 0.0), axis=0, keepdims=True)
            d1 = jnp.sum(jnp.where(eye, total[PW:, PW:], 0.0), axis=0, keepdims=True)
            den = jnp.where(tile_row == 0, d0, jnp.where(tile_row == 1, d1, 0.0))
            tile = split(den).astype(BF16)
            for at in range(VISITS):
                start = at * STRIP - HALO
                stop = start + SPAN
                if at == 0:
                    strip = jnp.concatenate([edge, total[0:stop, 0:PW]], axis=0)
                elif at == VISITS - 1:
                    strip = jnp.concatenate([total[start:PH, 0:PW], edge], axis=0)
                else:
                    strip = total[start:stop, 0:PW]
                sb[at, j, 0:SPAN, :] = strip.astype(BF16)
                sb[at, j, SPAN:, :] = tile

        @pl.loop(1, VISITS)
        def _(i):
            b_copy(part, lax.rem(v + i, VISITS)).start()

        pltpu.make_async_copy(
            strips_of(sb, v, part), strips_of(rbb, v, part), b_recv.at[part, v]
        ).start()

    def c_copy(j):
        return pltpu.make_async_remote_copy(
            src_ref=sc.at[j], dst_ref=rc.at[along],
            send_sem=c_send.at[j], recv_sem=c_recv.at[along],
            device_id={"patch": jnp.where(c == 0, patch_of(j, z, 0), patch_of(y, j, 1))},
            device_id_type=MESH,
        )

    def collect(part):
        for at in range(VISITS):
            pltpu.make_async_copy(
                strips_of(rbb, at, part), strips_of(rbb, at, part), b_recv.at[part, at]
            ).wait()

        for j in range(FIRST[part], FIRST[part] + PARTS[part]):
            total = rbb[0, j].astype(F32)
            for at in range(1, VISITS):
                total = total + rbb[at, j].astype(F32)
            sc[j, 0:SPAN, :] = total[0:SPAN].astype(BF16)
            sc[j, SPAN:, :] = split(joined(total[SPAN:])).astype(BF16)

            @pl.when(j == along)
            def _():
                pltpu.make_async_copy(sc.at[j], rc.at[along], c_recv.at[along]).start()

            @pl.when(j != along)
            def _():
                c_copy(j).start()

    add_up(0)
    for part in range(1, CHUNKS):
        add_up(part)
        collect(part - 1)
    collect(CHUNKS - 1)

    for part in range(CHUNKS):

        @pl.loop(0, 16)
        def _(message):
            @pl.when(message != here)
            def _():
                a_copy(message, part, z_slot, partner).wait_send()

        @pl.loop(1, VISITS)
        def _(i):
            b_copy(part, lax.rem(v + i, VISITS)).wait_send()

    total = jnp.zeros((LONG, PW), F32)
    for i in range(SIDE):
        pltpu.make_async_copy(rc.at[i], rc.at[i], c_recv.at[i]).wait()
        total = total + rc[i].astype(F32)
    sum_ref[0:SPAN, :] = total[0:SPAN]
    sum_ref[SPAN:, :] = joined(total[SPAN:])

    @pl.loop(0, SIDE)
    def _(j):
        @pl.when(j != along)
        def _():
            c_copy(j).wait_send()


def filter_kernel(sum_ref, taps_ref, coadd_ref, detection_ref, den_ref, pad_ref):
    v = lax.axis_index("visit")
    half = TD // 2
    pad_ref[...] = jnp.zeros_like(pad_ref)
    pad_ref[0:2, 6 : 6 + TD] = taps_ref[...].astype(F32)
    square = (PW, PW)
    lane, row = iota(square, 1), iota(square, 0)
    taps = jnp.broadcast_to(pad_ref[1:2, :], square)
    cols = pltpu.roll(taps, PW - half - 6, 1, stride=1, stride_axis=0)
    cols = jnp.where(jnp.abs(lane - row) <= half, cols, 0.0).astype(BF16)
    taps = jnp.broadcast_to(pad_ref[0:1, :], (STRIP, PW))
    rows = pltpu.roll(taps, HALO - half - 6, 1, stride=1, stride_axis=0).astype(BF16)
    den_ref[...] = jnp.zeros_like(den_ref)
    for a in range(2):
        column = jnp.broadcast_to(sum_ref[SPAN + a : SPAN + a + 1, :], square).T
        den_ref[HALO + a * PW : HALO + (a + 1) * PW, :] = column
    den = den_ref[pl.ds(pl.multiple_of(v * STRIP, STRIP), SPAN), :]
    coadd = sum_ref[0:SPAN, :] / (1.0 + den)
    coadd_ref[...] = coadd[HALO : HALO + STRIP]
    smoothed = jnp.dot(coadd.astype(BF16), cols, preferred_element_type=F32).astype(BF16)
    smoothed = jnp.concatenate([smoothed, jnp.zeros((PW - SPAN, PW), BF16)], axis=0)
    detection_ref[...] = jnp.dot(rows, smoothed, preferred_element_type=F32)


VMEM = pl.BlockSpec(memory_space=pltpu.VMEM)


def exchange(pieces, dest, offsets, kernel_index, weights, basis_col, basis_row, coef_table):
    dma = pltpu.SemaphoreType.DMA
    row = (1, PIECES)
    return pl.pallas_call(
        exchange_kernel,
        out_shape=pltpu.VMEM((LONG, PW), F32),
        in_specs=[pl.BlockSpec(memory_space=pl.ANY)] * 8,
        out_specs=VMEM,
        scratch_shapes=[
            pltpu.SMEM((PIECES,), I32),
            pltpu.SMEM(coef_table.shape[::-1], F32),
            pltpu.VMEM(row, I32),
            pltpu.VMEM(row, I32),
            pltpu.VMEM(row, BF16),
            pltpu.VMEM(basis_col.shape, BF16),
            pltpu.VMEM(basis_row.shape, BF16),
            pltpu.VMEM((PIECES, PR, PW), BF16),
            pltpu.VMEM((NB * PW, PW), BF16),
            pltpu.VMEM((NB, 4, 8, PW), F32),
            pltpu.VMEM((GROUP * PR, NB * PW), BF16),
            pltpu.VMEM((32, PW), F32),
            pltpu.VMEM((8, PW), F32),
            pltpu.VMEM((8, PW), I32),
            pltpu.SMEM((8, PW), I32),
            pltpu.VMEM((PIECES + 8, PR, PW), BF16),
            pltpu.VMEM((16, ROWS, PW), BF16),
            pltpu.VMEM((16, ROWS, PW), BF16),
            pltpu.VMEM((16, META, PW), F32),
            pltpu.VMEM((VISITS, SIDE, LONG, PW), BF16),
            pltpu.VMEM((VISITS, SIDE, LONG, PW), BF16),
            pltpu.VMEM((SIDE, LONG, PW), BF16),
            pltpu.VMEM((SIDE, LONG, PW), BF16),
            dma((7,)),
            dma(()),
            dma(()),
            dma((CHUNKS, 16)),
            dma((CHUNKS, 16)),
            dma((CHUNKS, VISITS)),
            dma((CHUNKS, VISITS)),
            dma((SIDE,)),
            dma((SIDE,)),
        ],
        compiler_params=pltpu.CompilerParams(collective_id=0, has_side_effects=True),
        name="exchange",
    )(
        kernel_index, coef_table.T, dest.reshape(row), offsets.reshape(row), weights.reshape(row),
        basis_col, basis_row, pieces,
    )


def finish(sums, det_taps):
    out = jax.ShapeDtypeStruct((STRIP, PW), F32)
    return pl.pallas_call(
        filter_kernel,
        out_shape=(out, out),
        in_specs=[VMEM, VMEM],
        out_specs=(VMEM, VMEM),
        scratch_shapes=[pltpu.VMEM((PH + 2 * HALO, PW), F32), pltpu.VMEM((8, PW), F32)],
        name="finish",
    )(pltpu.with_memory_space_constraint(sums, pltpu.VMEM), det_taps)


def shards(
    pieces, dest, offsets, kernel_index, weights, basis_col, basis_row, coef_table, det_taps
):
    sums = exchange(
        pieces, dest, offsets, kernel_index, weights, basis_col, basis_row, coef_table
    )
    return finish(sums, det_taps)


def solution(mesh):
    split = P(("patch", "visit"))
    in_specs = (
        P(("patch", "visit"), None, None),
        P(("patch", "visit"), None),
        split,
        split,
        split,
        P(),
        P(),
        P(),
        P(),
    )
    out_specs = (P(("patch", "visit"), None), P(("patch", "visit"), None))
    return jax.shard_map(shards, mesh=mesh, in_specs=in_specs, out_specs=out_specs, check_vma=False)
```

```python
import functools

import jax
import jax.numpy as jnp
from jax import lax
from jax.experimental import pallas as pl
from jax.experimental.pallas import tpu as pltpu
from jax.sharding import PartitionSpec as P

MESH = pl.DeviceIdType.MESH
F32 = jnp.float32
BF16 = jnp.bfloat16
I32 = jnp.int32

PIECES = 96
PR = 32
PW = 128
PH = 256
TAPS = 41
NB = 14
TD = 21
SIDE = 8
VISITS = 4
READY = 0
GROUP = 16
STRIP = PH // VISITS
HALO = 16
SPAN = STRIP + 2 * HALO
SLOTS = 16
META = 16
ROWS = META + SLOTS * PR
LONG = STRIP + 2 * HALO + 8
PARTS = (3, 2, 2, 1)
CHUNKS = len(PARTS)
FIRST = tuple(sum(PARTS[:part]) for part in range(CHUNKS))
EARLY = 2
ORDER = (4, 3, 5, 2, 6, 1, 7, 0)


def iota(shape, axis):
    return lax.broadcasted_iota(I32, shape, axis)


def chosen(index, values):
    result = jnp.full_like(index, values[-1])
    for at, value in enumerate(values[:-1]):
        result = jnp.where(index == at, value, result)
    return result


def tables(col_ref, row_ref, pad_ref, g_ref, r_ref):
    half = TAPS // 2
    pad_ref[...] = jnp.zeros_like(pad_ref)
    pad_ref[0:NB, 4 : 4 + TAPS] = col_ref[...].astype(F32)
    pad_ref[16 : 16 + NB, 4 : 4 + TAPS] = row_ref[...].astype(F32)
    band = jnp.abs(iota((PW, PW), 1) - iota((PW, PW), 0)) <= half
    row_lane = iota((PR, PW), 1)
    row_band = (jnp.abs(row_lane - iota((PR, PW), 0)) <= half) & (row_lane < PR)
    for b in range(NB):
        taps = jnp.broadcast_to(pad_ref[b : b + 1, :], (PW, PW))
        g = pltpu.roll(taps, PW - half - 4, 1, stride=1, stride_axis=0)
        g_ref[b * PW : (b + 1) * PW, :] = jnp.where(band, g, 0.0).astype(BF16)
        taps = jnp.broadcast_to(pad_ref[16 + b : 17 + b, :], (PR, PW))
        r = pltpu.roll(taps, PW - half - 4, 1, stride=1, stride_axis=0)
        r = jnp.where(row_band, r, 0.0)
        r = r + pltpu.roll(r, 32, 1) + pltpu.roll(r, 64, 1) + pltpu.roll(r, 96, 1)
        r_ref[b] = r.reshape(4, 8, PW)


def filters(taps_ref, pad_ref, cols_ref, rows_ref):
    half = TD // 2
    pad_ref[...] = jnp.zeros_like(pad_ref)
    pad_ref[0:2, 6 : 6 + TD] = taps_ref[...].astype(F32)
    square = (PW, PW)
    taps = jnp.broadcast_to(pad_ref[1:2, :], square)
    cols = pltpu.roll(taps, PW - half - 6, 1, stride=1, stride_axis=0)
    cols_ref[...] = jnp.where(
        jnp.abs(iota(square, 1) - iota(square, 0)) <= half, cols, 0.0
    ).astype(BF16)
    taps = jnp.broadcast_to(pad_ref[0:1, :], (STRIP, PW))
    rows = pltpu.roll(taps, HALO - half - 6, 1, stride=1, stride_axis=0)
    rows_ref[...] = rows.astype(BF16)


def plan(y, z, c, dest_ref, off_ref, weight_ref, plan_ref, padf_ref, stage_ref):
    plan_ref[...] = jnp.full_like(plan_ref, -1)
    plan_ref[0:1, 0:PIECES] = dest_ref[...]
    padf_ref[...] = jnp.zeros_like(padf_ref)
    padf_ref[0:1, 0:PIECES] = off_ref[...].astype(F32)
    padf_ref[1:2, 0:PIECES] = weight_ref[...].astype(F32)
    square = (PW, PW)
    lane, row = iota(square, 1), iota(square, 0)
    d = jnp.broadcast_to(plan_ref[0:1, :], square)
    d_t = d.T
    earlier = jnp.sum(jnp.where((d == d_t) & (row < lane), 1, 0), axis=0, keepdims=True)
    d1 = plan_ref[0:1, :]
    y_to, z_to, c_to = d1 >> 4, (d1 >> 1) & 7, d1 & 1
    distance = jnp.where(c_to == 0, z_to - z, y_to - y)
    distance = jnp.where(c_to == c, distance, -distance) & 7
    inner = jnp.where(c_to == 0, y_to, z_to)
    turn = chosen(distance, tuple(ORDER.index(o) for o in range(SIDE)))
    position = ((turn * 2 + c_to) * 8 + inner) * 2 + earlier
    lane1 = iota((1, PW), 1)
    position = jnp.where(lane1 < PIECES, position, 1024 + lane1)
    pos = jnp.broadcast_to(position, square)
    pos_t = pos.T
    rank = jnp.sum(jnp.where(pos_t < pos, 1, 0), axis=0, keepdims=True)
    rank_t = jnp.broadcast_to(rank, square).T
    order = jnp.sum(jnp.where(rank_t == lane, row, 0), axis=0, keepdims=True)
    plan_ref[0:1, :] = order
    for a in range(2):
        plan_ref[1 + a : 2 + a, :] = PIECES + jnp.sum(
            jnp.where(pos_t == lane + a * PW, rank_t - PIECES, 0), axis=0, keepdims=True
        )
    which = (lane // PR) & 1
    hot = jnp.concatenate(
        [jnp.where(pos == 2 * row + k, 1.0, 0.0).astype(BF16) for k in range(2)], axis=1
    )
    found = []
    for at in range(2):
        value = jnp.broadcast_to(padf_ref[at : at + 1, :], square).T
        value = jnp.concatenate(
            [jnp.where(which == k, value, 0.0).astype(BF16) for k in range(2)], axis=0
        )
        found.append(jnp.dot(hot, value, preferred_element_type=F32))
    target = found[0] + (lane & (PR - 1)).astype(F32)
    stage_ref[:, 0:META, :] = jnp.concatenate(
        [target.reshape(16, 8, PW), found[1].reshape(16, 8, PW)], axis=1
    ).astype(BF16)


def match_group(group, kind_s, coef_s, plan_s, x, r_ref, g_ref, y_ref, matched_ref):
    first = group * GROUP
    lane8 = iota((8, PW), 1)
    zeros = jnp.zeros((PR, PW), BF16)
    for quad in range(GROUP // 4):
        pieces = [plan_s[0, first + quad * 4 + j] for j in range(4)]
        kinds = [kind_s[n] for n in pieces]
        parts = []
        for b in range(NB):
            factor = jnp.where(
                lane8 < 64,
                jnp.where(lane8 < 32, coef_s[b, kinds[0]], coef_s[b, kinds[1]]),
                jnp.where(lane8 < 96, coef_s[b, kinds[2]], coef_s[b, kinds[3]]),
            )
            parts.append((r_ref[b] * factor[None]).reshape(PR, PW))
        row_kernel = jnp.concatenate(parts, axis=0).astype(BF16)
        images = [x[n] for n in pieces]
        for pair in range(2):
            rows = []
            for j in range(4):
                left = images[j] if j == 2 * pair else zeros
                right = images[j] if j == 2 * pair + 1 else zeros
                rows.append(jnp.concatenate([left, right], axis=1))
            both = jnp.concatenate(rows, axis=0)
            y = jnp.dot(row_kernel, both, preferred_element_type=F32).astype(BF16)
            for j in range(2):
                at = (quad * 4 + pair * 2 + j) * PR
                for b in range(NB):
                    y_ref[at : at + PR, b * PW : (b + 1) * PW] = y[
                        b * PR : (b + 1) * PR, j * PW : (j + 1) * PW
                    ]
    matched = jnp.dot(y_ref[...], g_ref[...], preferred_element_type=F32).astype(BF16)
    matched_ref[pl.ds(first, GROUP)] = matched.reshape(GROUP, PR, PW)


def exchange_kernel(
    kind_in, coef_in, dest_in, off_in, weight_in, col_in, row_in, taps_in, pieces_ref,
    coadd_ref, detection_ref,
    sum_ref, den_ref, cols_ref, rows_ref, taps_ref,
    kind_s, coef_s, dest_ref, off_ref, weight_ref, col_ref, row_ref, x, g_ref, r_ref, y_ref, pad_ref, padf_ref, plan_ref, plan_s, matched_ref, stage_ref,
    rb, mf, sb, rbb, sc, rc,
    in_sem, x_sem, plan_sem, a_send, a_recv, b_send, b_recv, c_send, c_recv,
):
    p = lax.axis_index("patch")
    v = lax.axis_index("visit")
    c = lax.rem(p, 2)
    z = lax.rem(p // 2, SIDE)
    y = p // (2 * SIDE)
    along = jnp.where(c == 0, y, z)

    def patch_of(y_at, z_at, c_at):
        return (y_at * SIDE + z_at) * 2 + c_at

    small = [
        pltpu.make_async_copy(source, target, in_sem.at[at])
        for at, (source, target) in enumerate(
            (
                (dest_in, dest_ref), (off_in, off_ref), (weight_in, weight_ref),
                (col_in, col_ref), (row_in, row_ref), (kind_in, kind_s), (coef_in, coef_s),
                (taps_in, taps_ref),
            )
        )
    ]
    for copy in small:
        copy.start()
    x_copy = pltpu.make_async_copy(pieces_ref, x, x_sem)
    x_copy.start()

    barrier = pltpu.get_barrier_semaphore()

    def greet(target):
        pl.semaphore_signal(barrier, inc=1, device_id={"patch": target}, device_id_type=MESH)

    @pl.loop(1, SIDE)
    def _(i):
        for core in range(2):
            greet(patch_of(y, lax.rem(z + i, SIDE), core))
            greet(patch_of(lax.rem(y + i, SIDE), z, core))

    greet(patch_of(y, z, 1 - c))

    @pl.loop(1, VISITS)
    def _(i):
        pl.semaphore_signal(
            barrier, inc=1, device_id={"visit": lax.rem(v + i, VISITS)}, device_id_type=MESH
        )

    for copy in small:
        copy.wait()
    plan(y, z, c, dest_ref, off_ref, weight_ref, plan_ref, padf_ref, stage_ref)
    plan_copy = pltpu.make_async_copy(plan_ref, plan_s, plan_sem)
    plan_copy.start()
    tables(col_ref, row_ref, pad_ref, g_ref, r_ref)
    filters(taps_ref, pad_ref, cols_ref, rows_ref)
    den_ref[...] = jnp.zeros_like(den_ref)
    matched_ref[PIECES:, :, :] = jnp.zeros((8, PR, PW), BF16)
    plan_copy.wait()
    x_copy.wait()

    def part_of(ref, at, part):
        if part == 0:
            return ref.at[at, pl.ds(0, META + PARTS[0] * 64)]
        return ref.at[at, pl.ds(META + FIRST[part] * 64, PARTS[part] * 64)]

    def a_copy(message, part, slot, target):
        return pltpu.make_async_remote_copy(
            src_ref=part_of(stage_ref, message, part), dst_ref=part_of(rb, slot, part),
            send_sem=a_send.at[part, message], recv_sem=a_recv.at[part, slot],
            device_id={"patch": target}, device_id_type=MESH,
        )

    z_slot = z * 2 + c
    y_slot = y * 2 + c
    partner = patch_of(y, z, 1 - c)
    here = 2 * (SIDE - 1) + c

    def fill(message):
        for s in range(SLOTS):
            r = plan_s[1 + message // 8, (message % 8) * SLOTS + s]
            stage_ref[message, META + s * PR : META + (s + 1) * PR, :] = matched_ref[r]

    def send(message, part):
        even = lax.rem(message, 2) == 0
        distance = chosen(message // 2, ORDER)
        distance = jnp.where(lax.rem(message, 2) == c, distance, lax.rem(SIDE - distance, SIDE))
        target = jnp.where(
            even,
            patch_of(y, lax.rem(z + distance, SIDE), 0),
            patch_of(lax.rem(y + distance, SIDE), z, 1),
        )
        slot = jnp.where(even, z_slot, y_slot)

        @pl.when(message != here)
        def _():
            a_copy(message, part, slot, target).start()

        @pl.when(message == here)
        def _():
            pltpu.make_async_copy(
                part_of(stage_ref, message, part), part_of(rb, slot, part), a_recv.at[part, slot]
            ).start()

    def send_fixed(message, part):
        core = message % 2
        distance = ORDER[message // 2]
        step = jnp.where(c == core, distance, (SIDE - distance) % SIDE)
        if core == 0:
            target, slot = patch_of(y, lax.rem(z + step, SIDE), 0), z_slot
        else:
            target, slot = patch_of(lax.rem(y + step, SIDE), z, 1), y_slot
        if distance:
            a_copy(message, part, slot, target).start()
        else:

            @pl.when(c != core)
            def _():
                a_copy(message, part, slot, target).start()

            @pl.when(c == core)
            def _():
                pltpu.make_async_copy(
                    part_of(stage_ref, message, part), part_of(rb, slot, part),
                    a_recv.at[part, slot],
                ).start()

    groups = PIECES // GROUP

    @pl.loop(0, groups)
    def _(group):
        match_group(group, kind_s, coef_s, plan_s, x, r_ref, g_ref, y_ref, matched_ref)
        fill(group)

        @pl.when(group == READY)
        def _():
            pl.semaphore_wait(barrier, 4 * (SIDE - 1) + 1 + VISITS - 1)

            @pl.loop(0, READY)
            def _(message):
                for part in range(EARLY):
                    send(message, part)

        @pl.when(group >= READY)
        def _():
            for part in range(EARLY):
                send(group, part)

    for part in range(CHUNKS):
        for message in range(groups if part < EARLY else 0, 16):
            if part == 0:
                fill(message)
            send_fixed(message, part)

    row_f = iota((PH, PW), 0).astype(F32)
    low = iota((1, PW), 1) < 64
    eye = iota((PW, PW), 0) == iota((PW, PW), 1)
    tile_row = iota((8, PW), 0)
    ones = jnp.ones((4 * 64, PW), BF16)
    edge = jnp.zeros((HALO, PW), F32)

    def split(den):
        high = den.astype(BF16).astype(F32)
        return jnp.where(tile_row < 4, high, pltpu.roll(den - high, 4, 0))

    def joined(tile):
        return tile + pltpu.roll(tile, 4, 0)

    def strips_of(ref, at, part):
        return ref.at[at, pl.ds(FIRST[part], PARTS[part])]

    def b_copy(part, at):
        return pltpu.make_async_remote_copy(
            src_ref=strips_of(sb, at, part), dst_ref=strips_of(rbb, v, part),
            send_sem=b_send.at[part, at], recv_sem=b_recv.at[part, v],
            device_id={"visit": at}, device_id_type=MESH,
        )

    def add_up(part):
        @pl.loop(0, 16)
        def _(s):
            a_copy(s, part, s, partner).wait_recv()

        if part == 0:
            mf[...] = rb[:, 0:META, :].astype(F32)

        @pl.loop(FIRST[part], FIRST[part] + PARTS[part])
        def _(j):
            total = jnp.zeros((PH, 2 * PW), F32)
            for four in range(4):
                places = []
                blocks = []
                for pair in range(2):
                    s = four * 4 + pair * 2
                    t = jnp.where(low, mf[s, pl.ds(j, 1), :], mf[s + 1, pl.ds(j, 1), :])
                    w = jnp.where(low, mf[s, pl.ds(8 + j, 1), :], mf[s + 1, pl.ds(8 + j, 1), :])
                    places.append(jnp.where(row_f == t, w, 0.0).astype(BF16))
                    for k in range(2):
                        blocks.append(rb[s + k, pl.ds(pl.multiple_of(META + 64 * j, 16), 64), :])
                place = jnp.concatenate(places, axis=1)
                block = jnp.concatenate([jnp.concatenate(blocks, axis=0), ones], axis=1)
                total = total + jnp.dot(place, block, preferred_element_type=F32)
            d0 = jnp.sum(jnp.where(eye, total[0:PW, PW:], 0.0), axis=0, keepdims=True)
            d1 = jnp.sum(jnp.where(eye, total[PW:, PW:], 0.0), axis=0, keepdims=True)
            den = jnp.where(tile_row == 0, d0, jnp.where(tile_row == 1, d1, 0.0))
            tile = split(den).astype(BF16)
            for at in range(VISITS):
                start = at * STRIP - HALO
                stop = start + SPAN
                if at == 0:
                    strip = jnp.concatenate([edge, total[0:stop, 0:PW]], axis=0)
                elif at == VISITS - 1:
                    strip = jnp.concatenate([total[start:PH, 0:PW], edge], axis=0)
                else:
                    strip = total[start:stop, 0:PW]
                sb[at, j, 0:SPAN, :] = strip.astype(BF16)
                sb[at, j, SPAN:, :] = tile

        @pl.loop(1, VISITS)
        def _(i):
            b_copy(part, lax.rem(v + i, VISITS)).start()

        pltpu.make_async_copy(
            strips_of(sb, v, part), strips_of(rbb, v, part), b_recv.at[part, v]
        ).start()

    def c_copy(j):
        return pltpu.make_async_remote_copy(
            src_ref=sc.at[j], dst_ref=rc.at[along],
            send_sem=c_send.at[j], recv_sem=c_recv.at[along],
            device_id={"patch": jnp.where(c == 0, patch_of(j, z, 0), patch_of(y, j, 1))},
            device_id_type=MESH,
        )

    def collect(part):
        for at in range(VISITS):
            pltpu.make_async_copy(
                strips_of(rbb, at, part), strips_of(rbb, at, part), b_recv.at[part, at]
            ).wait()

        for j in range(FIRST[part], FIRST[part] + PARTS[part]):
            total = rbb[0, j].astype(F32)
            for at in range(1, VISITS):
                total = total + rbb[at, j].astype(F32)
            sc[j, 0:SPAN, :] = total[0:SPAN].astype(BF16)
            sc[j, SPAN:, :] = split(joined(total[SPAN:])).astype(BF16)

            @pl.when(j == along)
            def _():
                pltpu.make_async_copy(sc.at[j], rc.at[along], c_recv.at[along]).start()

            @pl.when(j != along)
            def _():
                c_copy(j).start()

    add_up(0)
    for part in range(1, CHUNKS):
        add_up(part)
        collect(part - 1)
    collect(CHUNKS - 1)

    for part in range(CHUNKS):

        @pl.loop(0, 16)
        def _(message):
            @pl.when(message != here)
            def _():
                a_copy(message, part, z_slot, partner).wait_send()

        @pl.loop(1, VISITS)
        def _(i):
            b_copy(part, lax.rem(v + i, VISITS)).wait_send()

    total = jnp.zeros((LONG, PW), F32)
    for i in range(SIDE):
        pltpu.make_async_copy(rc.at[i], rc.at[i], c_recv.at[i]).wait()
        total = total + rc[i].astype(F32)
    sum_ref[...] = joined(total[SPAN:])
    for a in range(2):
        column = jnp.broadcast_to(sum_ref[a : a + 1, :], (PW, PW)).T
        den_ref[HALO + a * PW : HALO + (a + 1) * PW, :] = column
    den = den_ref[pl.ds(pl.multiple_of(v * STRIP, STRIP), SPAN), :]
    coadd = total[0:SPAN] / (1.0 + den)
    coadd_ref[...] = coadd[HALO : HALO + STRIP]
    smoothed = jnp.dot(coadd.astype(BF16), cols_ref[...], preferred_element_type=F32).astype(BF16)
    smoothed = jnp.concatenate([smoothed, jnp.zeros((PW - SPAN, PW), BF16)], axis=0)
    detection_ref[...] = jnp.dot(rows_ref[...], smoothed, preferred_element_type=F32)

    @pl.loop(0, SIDE)
    def _(j):
        @pl.when(j != along)
        def _():
            c_copy(j).wait_send()


VMEM = pl.BlockSpec(memory_space=pltpu.VMEM)


def exchange(
    pieces, dest, offsets, kernel_index, weights, basis_col, basis_row, coef_table, det_taps
):
    dma = pltpu.SemaphoreType.DMA
    row = (1, PIECES)
    return pl.pallas_call(
        exchange_kernel,
        out_shape=(pltpu.VMEM((STRIP, PW), F32), pltpu.VMEM((STRIP, PW), F32)),
        in_specs=[pl.BlockSpec(memory_space=pl.ANY)] * 9,
        out_specs=(VMEM, VMEM),
        scratch_shapes=[
            pltpu.VMEM((8, PW), F32),
            pltpu.VMEM((PH + 2 * HALO, PW), F32),
            pltpu.VMEM((PW, PW), BF16),
            pltpu.VMEM((STRIP, PW), BF16),
            pltpu.VMEM(det_taps.shape, BF16),
            pltpu.SMEM((PIECES,), I32),
            pltpu.SMEM(coef_table.shape[::-1], F32),
            pltpu.VMEM(row, I32),
            pltpu.VMEM(row, I32),
            pltpu.VMEM(row, BF16),
            pltpu.VMEM(basis_col.shape, BF16),
            pltpu.VMEM(basis_row.shape, BF16),
            pltpu.VMEM((PIECES, PR, PW), BF16),
            pltpu.VMEM((NB * PW, PW), BF16),
            pltpu.VMEM((NB, 4, 8, PW), F32),
            pltpu.VMEM((GROUP * PR, NB * PW), BF16),
            pltpu.VMEM((32, PW), F32),
            pltpu.VMEM((8, PW), F32),
            pltpu.VMEM((8, PW), I32),
            pltpu.SMEM((8, PW), I32),
            pltpu.VMEM((PIECES + 8, PR, PW), BF16),
            pltpu.VMEM((16, ROWS, PW), BF16),
            pltpu.VMEM((16, ROWS, PW), BF16),
            pltpu.VMEM((16, META, PW), F32),
            pltpu.VMEM((VISITS, SIDE, LONG, PW), BF16),
            pltpu.VMEM((VISITS, SIDE, LONG, PW), BF16),
            pltpu.VMEM((SIDE, LONG, PW), BF16),
            pltpu.VMEM((SIDE, LONG, PW), BF16),
            dma((8,)),
            dma(()),
            dma(()),
            dma((CHUNKS, 16)),
            dma((CHUNKS, 16)),
            dma((CHUNKS, VISITS)),
            dma((CHUNKS, VISITS)),
            dma((SIDE,)),
            dma((SIDE,)),
        ],
        compiler_params=pltpu.CompilerParams(collective_id=0, has_side_effects=True),
        name="exchange",
    )(
        kernel_index, coef_table.T, dest.reshape(row), offsets.reshape(row), weights.reshape(row),
        basis_col, basis_row, det_taps, pieces,
    )


def shards(
    pieces, dest, offsets, kernel_index, weights, basis_col, basis_row, coef_table, det_taps
):
    return exchange(
        pieces, dest, offsets, kernel_index, weights, basis_col, basis_row, coef_table, det_taps
    )


def solution(mesh):
    split = P(("patch", "visit"))
    in_specs = (
        P(("patch", "visit"), None, None),
        P(("patch", "visit"), None),
        split,
        split,
        split,
        P(),
        P(),
        P(),
        P(),
    )
    out_specs = (P(("patch", "visit"), None), P(("patch", "visit"), None))
    return jax.shard_map(shards, mesh=mesh, in_specs=in_specs, out_specs=out_specs, check_vma=False)
```

```python
import functools

import jax
import jax.numpy as jnp
from jax import lax
from jax.experimental import pallas as pl
from jax.experimental.pallas import tpu as pltpu
from jax.sharding import PartitionSpec as P

MESH = pl.DeviceIdType.MESH
F32 = jnp.float32
BF16 = jnp.bfloat16
I32 = jnp.int32

PIECES = 96
PR = 32
PW = 128
PH = 256
TAPS = 41
NB = 14
TD = 21
SIDE = 8
VISITS = 4
READY = 0
GROUP = 16
STRIP = PH // VISITS
HALO = 16
SPAN = STRIP + 2 * HALO
SLOTS = 16
META = 16
ROWS = META + SLOTS * PR
LONG = STRIP + 2 * HALO + 8
PARTS = (4, 2, 2)
CHUNKS = len(PARTS)
FIRST = tuple(sum(PARTS[:part]) for part in range(CHUNKS))
EARLY = 1
ORDER = (4, 3, 5, 2, 6, 1, 7, 0)


def iota(shape, axis):
    return lax.broadcasted_iota(I32, shape, axis)


def chosen(index, values):
    result = jnp.full_like(index, values[-1])
    for at, value in enumerate(values[:-1]):
        result = jnp.where(index == at, value, result)
    return result


def tables(col_ref, row_ref, pad_ref, g_ref, r_ref):
    half = TAPS // 2
    pad_ref[...] = jnp.zeros_like(pad_ref)
    pad_ref[0:NB, 4 : 4 + TAPS] = col_ref[...].astype(F32)
    pad_ref[16 : 16 + NB, 4 : 4 + TAPS] = row_ref[...].astype(F32)
    band = jnp.abs(iota((PW, PW), 1) - iota((PW, PW), 0)) <= half
    row_lane = iota((PR, PW), 1)
    row_band = (jnp.abs(row_lane - iota((PR, PW), 0)) <= half) & (row_lane < PR)
    for b in range(NB):
        taps = jnp.broadcast_to(pad_ref[b : b + 1, :], (PW, PW))
        g = pltpu.roll(taps, PW - half - 4, 1, stride=1, stride_axis=0)
        g_ref[b * PW : (b + 1) * PW, :] = jnp.where(band, g, 0.0).astype(BF16)
        taps = jnp.broadcast_to(pad_ref[16 + b : 17 + b, :], (PR, PW))
        r = pltpu.roll(taps, PW - half - 4, 1, stride=1, stride_axis=0)
        r = jnp.where(row_band, r, 0.0)
        r = r + pltpu.roll(r, 32, 1) + pltpu.roll(r, 64, 1) + pltpu.roll(r, 96, 1)
        r_ref[b] = r.reshape(4, 8, PW)


def filters(taps_ref, pad_ref, cols_ref, rows_ref):
    half = TD // 2
    pad_ref[...] = jnp.zeros_like(pad_ref)
    pad_ref[0:2, 6 : 6 + TD] = taps_ref[...].astype(F32)
    square = (PW, PW)
    taps = jnp.broadcast_to(pad_ref[1:2, :], square)
    cols = pltpu.roll(taps, PW - half - 6, 1, stride=1, stride_axis=0)
    cols_ref[...] = jnp.where(
        jnp.abs(iota(square, 1) - iota(square, 0)) <= half, cols, 0.0
    ).astype(BF16)
    taps = jnp.broadcast_to(pad_ref[0:1, :], (STRIP, PW))
    rows = pltpu.roll(taps, HALO - half - 6, 1, stride=1, stride_axis=0)
    rows_ref[...] = rows.astype(BF16)


def plan(y, z, c, dest_ref, off_ref, weight_ref, plan_ref, padf_ref, stage_ref):
    plan_ref[...] = jnp.full_like(plan_ref, -1)
    plan_ref[0:1, 0:PIECES] = dest_ref[...]
    padf_ref[...] = jnp.zeros_like(padf_ref)
    padf_ref[0:1, 0:PIECES] = off_ref[...].astype(F32)
    padf_ref[1:2, 0:PIECES] = weight_ref[...].astype(F32)
    square = (PW, PW)
    lane, row = iota(square, 1), iota(square, 0)
    d = jnp.broadcast_to(plan_ref[0:1, :], square)
    d_t = d.T
    earlier = jnp.sum(jnp.where((d == d_t) & (row < lane), 1, 0), axis=0, keepdims=True)
    d1 = plan_ref[0:1, :]
    y_to, z_to, c_to = d1 >> 4, (d1 >> 1) & 7, d1 & 1
    distance = jnp.where(c_to == 0, z_to - z, y_to - y)
    distance = jnp.where(c_to == c, distance, -distance) & 7
    inner = jnp.where(c_to == 0, y_to, z_to)
    turn = chosen(distance, tuple(ORDER.index(o) for o in range(SIDE)))
    position = ((turn * 2 + c_to) * 8 + inner) * 2 + earlier
    lane1 = iota((1, PW), 1)
    position = jnp.where(lane1 < PIECES, position, 1024 + lane1)
    pos = jnp.broadcast_to(position, square)
    pos_t = pos.T
    rank = jnp.sum(jnp.where(pos_t < pos, 1, 0), axis=0, keepdims=True)
    rank_t = jnp.broadcast_to(rank, square).T
    order = jnp.sum(jnp.where(rank_t == lane, row, 0), axis=0, keepdims=True)
    plan_ref[0:1, :] = order
    for a in range(2):
        plan_ref[1 + a : 2 + a, :] = PIECES + jnp.sum(
            jnp.where(pos_t == lane + a * PW, rank_t - PIECES, 0), axis=0, keepdims=True
        )
    which = (lane // PR) & 1
    hot = jnp.concatenate(
        [jnp.where(pos == 2 * row + k, 1.0, 0.0).astype(BF16) for k in range(2)], axis=1
    )
    found = []
    for at in range(2):
        value = jnp.broadcast_to(padf_ref[at : at + 1, :], square).T
        value = jnp.concatenate(
            [jnp.where(which == k, value, 0.0).astype(BF16) for k in range(2)], axis=0
        )
        found.append(jnp.dot(hot, value, preferred_element_type=F32))
    target = found[0] + (lane & (PR - 1)).astype(F32)
    stage_ref[:, 0:META, :] = jnp.concatenate(
        [target.reshape(16, 8, PW), found[1].reshape(16, 8, PW)], axis=1
    ).astype(BF16)


def match_group(group, kind_s, coef_s, plan_s, x, r_ref, g_ref, y_ref, matched_ref):
    first = group * GROUP
    lane8 = iota((8, PW), 1)
    zeros = jnp.zeros((PR, PW), BF16)
    for quad in range(GROUP // 4):
        pieces = [plan_s[0, first + quad * 4 + j] for j in range(4)]
        kinds = [kind_s[n] for n in pieces]
        parts = []
        for b in range(NB):
            factor = jnp.where(
                lane8 < 64,
                jnp.where(lane8 < 32, coef_s[b, kinds[0]], coef_s[b, kinds[1]]),
                jnp.where(lane8 < 96, coef_s[b, kinds[2]], coef_s[b, kinds[3]]),
            )
            parts.append((r_ref[b] * factor[None]).reshape(PR, PW))
        row_kernel = jnp.concatenate(parts, axis=0).astype(BF16)
        images = [x[n] for n in pieces]
        for pair in range(2):
            rows = []
            for j in range(4):
                left = images[j] if j == 2 * pair else zeros
                right = images[j] if j == 2 * pair + 1 else zeros
                rows.append(jnp.concatenate([left, right], axis=1))
            both = jnp.concatenate(rows, axis=0)
            y = jnp.dot(row_kernel, both, preferred_element_type=F32).astype(BF16)
            for j in range(2):
                at = (quad * 4 + pair * 2 + j) * PR
                for b in range(NB):
                    y_ref[at : at + PR, b * PW : (b + 1) * PW] = y[
                        b * PR : (b + 1) * PR, j * PW : (j + 1) * PW
                    ]
    matched = jnp.dot(y_ref[...], g_ref[...], preferred_element_type=F32).astype(BF16)
    matched_ref[pl.ds(first, GROUP)] = matched.reshape(GROUP, PR, PW)


def exchange_kernel(
    kind_in, coef_in, dest_in, off_in, weight_in, col_in, row_in, taps_in, pieces_ref,
    coadd_ref, detection_ref,
    sum_ref, den_ref, cols_ref, rows_ref, taps_ref,
    kind_s, coef_s, dest_ref, off_ref, weight_ref, col_ref, row_ref, x, g_ref, r_ref, y_ref, pad_ref, padf_ref, plan_ref, plan_s, matched_ref, stage_ref,
    rb, mf, sb, rbb, sc, rc,
    in_sem, x_sem, plan_sem, a_send, a_recv, b_send, b_recv, c_send, c_recv,
):
    p = lax.axis_index("patch")
    v = lax.axis_index("visit")
    c = lax.rem(p, 2)
    z = lax.rem(p // 2, SIDE)
    y = p // (2 * SIDE)
    along = jnp.where(c == 0, y, z)

    def patch_of(y_at, z_at, c_at):
        return (y_at * SIDE + z_at) * 2 + c_at

    small = [
        pltpu.make_async_copy(source, target, in_sem.at[at])
        for at, (source, target) in enumerate(
            (
                (dest_in, dest_ref), (off_in, off_ref), (weight_in, weight_ref),
                (col_in, col_ref), (row_in, row_ref), (kind_in, kind_s), (coef_in, coef_s),
                (taps_in, taps_ref),
            )
        )
    ]
    for copy in small:
        copy.start()
    x_copy = pltpu.make_async_copy(pieces_ref, x, x_sem)
    x_copy.start()

    barrier = pltpu.get_barrier_semaphore()

    def greet(target):
        pl.semaphore_signal(barrier, inc=1, device_id={"patch": target}, device_id_type=MESH)

    @pl.loop(1, SIDE)
    def _(i):
        for core in range(2):
            greet(patch_of(y, lax.rem(z + i, SIDE), core))
            greet(patch_of(lax.rem(y + i, SIDE), z, core))

    greet(patch_of(y, z, 1 - c))

    @pl.loop(1, VISITS)
    def _(i):
        pl.semaphore_signal(
            barrier, inc=1, device_id={"visit": lax.rem(v + i, VISITS)}, device_id_type=MESH
        )

    for copy in small:
        copy.wait()
    plan(y, z, c, dest_ref, off_ref, weight_ref, plan_ref, padf_ref, stage_ref)
    plan_copy = pltpu.make_async_copy(plan_ref, plan_s, plan_sem)
    plan_copy.start()
    tables(col_ref, row_ref, pad_ref, g_ref, r_ref)
    filters(taps_ref, pad_ref, cols_ref, rows_ref)
    den_ref[...] = jnp.zeros_like(den_ref)
    matched_ref[PIECES:, :, :] = jnp.zeros((8, PR, PW), BF16)
    plan_copy.wait()
    x_copy.wait()

    def part_of(ref, at, part):
        if part == 0:
            return ref.at[at, pl.ds(0, META + PARTS[0] * 64)]
        return ref.at[at, pl.ds(META + FIRST[part] * 64, PARTS[part] * 64)]

    def a_copy(message, part, slot, target):
        return pltpu.make_async_remote_copy(
            src_ref=part_of(stage_ref, message, part), dst_ref=part_of(rb, slot, part),
            send_sem=a_send.at[part, message], recv_sem=a_recv.at[part, slot],
            device_id={"patch": target}, device_id_type=MESH,
        )

    z_slot = z * 2 + c
    y_slot = y * 2 + c
    partner = patch_of(y, z, 1 - c)
    here = 2 * (SIDE - 1) + c

    def fill(message):
        for s in range(SLOTS):
            r = plan_s[1 + message // 8, (message % 8) * SLOTS + s]
            stage_ref[message, META + s * PR : META + (s + 1) * PR, :] = matched_ref[r]

    def send(message, part):
        even = lax.rem(message, 2) == 0
        distance = chosen(message // 2, ORDER)
        distance = jnp.where(lax.rem(message, 2) == c, distance, lax.rem(SIDE - distance, SIDE))
        target = jnp.where(
            even,
            patch_of(y, lax.rem(z + distance, SIDE), 0),
            patch_of(lax.rem(y + distance, SIDE), z, 1),
        )
        slot = jnp.where(even, z_slot, y_slot)

        @pl.when(message != here)
        def _():
            a_copy(message, part, slot, target).start()

        @pl.when(message == here)
        def _():
            pltpu.make_async_copy(
                part_of(stage_ref, message, part), part_of(rb, slot, part), a_recv.at[part, slot]
            ).start()

    def send_fixed(message, part):
        core = message % 2
        distance = ORDER[message // 2]
        step = jnp.where(c == core, distance, (SIDE - distance) % SIDE)
        if core == 0:
            target, slot = patch_of(y, lax.rem(z + step, SIDE), 0), z_slot
        else:
            target, slot = patch_of(lax.rem(y + step, SIDE), z, 1), y_slot
        if distance:
            a_copy(message, part, slot, target).start()
        else:

            @pl.when(c != core)
            def _():
                a_copy(message, part, slot, target).start()

            @pl.when(c == core)
            def _():
                pltpu.make_async_copy(
                    part_of(stage_ref, message, part), part_of(rb, slot, part),
                    a_recv.at[part, slot],
                ).start()

    groups = PIECES // GROUP

    @pl.loop(0, groups)
    def _(group):
        match_group(group, kind_s, coef_s, plan_s, x, r_ref, g_ref, y_ref, matched_ref)
        fill(group)

        @pl.when(group == READY)
        def _():
            pl.semaphore_wait(barrier, 4 * (SIDE - 1) + 1 + VISITS - 1)

            @pl.loop(0, READY)
            def _(message):
                for part in range(EARLY):
                    send(message, part)

        @pl.when(group >= READY)
        def _():
            for part in range(EARLY):
                send(group, part)

    for part in range(CHUNKS):
        for message in range(groups if part < EARLY else 0, 16):
            if part == 0:
                fill(message)
            send_fixed(message, part)

    row_f = iota((PH, PW), 0).astype(F32)
    low = iota((1, PW), 1) < 64
    eye = iota((PW, PW), 0) == iota((PW, PW), 1)
    tile_row = iota((8, PW), 0)
    ones = jnp.ones((4 * 64, PW), BF16)
    edge = jnp.zeros((HALO, PW), F32)

    def split(den):
        high = den.astype(BF16).astype(F32)
        return jnp.where(tile_row < 4, high, pltpu.roll(den - high, 4, 0))

    def joined(tile):
        return tile + pltpu.roll(tile, 4, 0)

    def strips_of(ref, at, part):
        return ref.at[at, pl.ds(FIRST[part], PARTS[part])]

    def b_copy(part, at):
        return pltpu.make_async_remote_copy(
            src_ref=strips_of(sb, at, part), dst_ref=strips_of(rbb, v, part),
            send_sem=b_send.at[part, at], recv_sem=b_recv.at[part, v],
            device_id={"visit": at}, device_id_type=MESH,
        )

    def add_up(part):
        @pl.loop(0, 16)
        def _(s):
            a_copy(s, part, s, partner).wait_recv()

        if part == 0:
            mf[...] = rb[:, 0:META, :].astype(F32)

        @pl.loop(FIRST[part], FIRST[part] + PARTS[part])
        def _(j):
            total = jnp.zeros((PH, 2 * PW), F32)
            for four in range(4):
                places = []
                blocks = []
                for pair in range(2):
                    s = four * 4 + pair * 2
                    t = jnp.where(low, mf[s, pl.ds(j, 1), :], mf[s + 1, pl.ds(j, 1), :])
                    w = jnp.where(low, mf[s, pl.ds(8 + j, 1), :], mf[s + 1, pl.ds(8 + j, 1), :])
                    places.append(jnp.where(row_f == t, w, 0.0).astype(BF16))
                    for k in range(2):
                        blocks.append(rb[s + k, pl.ds(pl.multiple_of(META + 64 * j, 16), 64), :])
                place = jnp.concatenate(places, axis=1)
                block = jnp.concatenate([jnp.concatenate(blocks, axis=0), ones], axis=1)
                total = total + jnp.dot(place, block, preferred_element_type=F32)
            d0 = jnp.sum(jnp.where(eye, total[0:PW, PW:], 0.0), axis=0, keepdims=True)
            d1 = jnp.sum(jnp.where(eye, total[PW:, PW:], 0.0), axis=0, keepdims=True)
            den = jnp.where(tile_row == 0, d0, jnp.where(tile_row == 1, d1, 0.0))
            tile = split(den).astype(BF16)
            for at in range(VISITS):
                start = at * STRIP - HALO
                stop = start + SPAN
                if at == 0:
                    strip = jnp.concatenate([edge, total[0:stop, 0:PW]], axis=0)
                elif at == VISITS - 1:
                    strip = jnp.concatenate([total[start:PH, 0:PW], edge], axis=0)
                else:
                    strip = total[start:stop, 0:PW]
                sb[at, j, 0:SPAN, :] = strip.astype(BF16)
                sb[at, j, SPAN:, :] = tile

        @pl.loop(1, VISITS)
        def _(i):
            b_copy(part, lax.rem(v + i, VISITS)).start()

        pltpu.make_async_copy(
            strips_of(sb, v, part), strips_of(rbb, v, part), b_recv.at[part, v]
        ).start()

    def c_copy(j):
        return pltpu.make_async_remote_copy(
            src_ref=sc.at[j], dst_ref=rc.at[along],
            send_sem=c_send.at[j], recv_sem=c_recv.at[along],
            device_id={"patch": jnp.where(c == 0, patch_of(j, z, 0), patch_of(y, j, 1))},
            device_id_type=MESH,
        )

    def collect(part):
        for at in range(VISITS):
            pltpu.make_async_copy(
                strips_of(rbb, at, part), strips_of(rbb, at, part), b_recv.at[part, at]
            ).wait()

        for j in range(FIRST[part], FIRST[part] + PARTS[part]):
            total = rbb[0, j].astype(F32)
            for at in range(1, VISITS):
                total = total + rbb[at, j].astype(F32)
            sc[j, 0:SPAN, :] = total[0:SPAN].astype(BF16)
            sc[j, SPAN:, :] = split(joined(total[SPAN:])).astype(BF16)

            @pl.when(j == along)
            def _():
                pltpu.make_async_copy(sc.at[j], rc.at[along], c_recv.at[along]).start()

            @pl.when(j != along)
            def _():
                c_copy(j).start()

    add_up(0)
    for part in range(1, CHUNKS):
        add_up(part)
        collect(part - 1)
    collect(CHUNKS - 1)

    for part in range(CHUNKS):

        @pl.loop(0, 16)
        def _(message):
            @pl.when(message != here)
            def _():
                a_copy(message, part, z_slot, partner).wait_send()

        @pl.loop(1, VISITS)
        def _(i):
            b_copy(part, lax.rem(v + i, VISITS)).wait_send()

    total = jnp.zeros((LONG, PW), F32)
    for i in range(SIDE):
        pltpu.make_async_copy(rc.at[i], rc.at[i], c_recv.at[i]).wait()
        total = total + rc[i].astype(F32)
    sum_ref[...] = joined(total[SPAN:])
    for a in range(2):
        column = jnp.broadcast_to(sum_ref[a : a + 1, :], (PW, PW)).T
        den_ref[HALO + a * PW : HALO + (a + 1) * PW, :] = column
    den = den_ref[pl.ds(pl.multiple_of(v * STRIP, STRIP), SPAN), :]
    coadd = total[0:SPAN] / (1.0 + den)
    coadd_ref[...] = coadd[HALO : HALO + STRIP]
    smoothed = jnp.dot(coadd.astype(BF16), cols_ref[...], preferred_element_type=F32).astype(BF16)
    smoothed = jnp.concatenate([smoothed, jnp.zeros((PW - SPAN, PW), BF16)], axis=0)
    detection_ref[...] = jnp.dot(rows_ref[...], smoothed, preferred_element_type=F32)

    @pl.loop(0, SIDE)
    def _(j):
        @pl.when(j != along)
        def _():
            c_copy(j).wait_send()


VMEM = pl.BlockSpec(memory_space=pltpu.VMEM)


def exchange(
    pieces, dest, offsets, kernel_index, weights, basis_col, basis_row, coef_table, det_taps
):
    dma = pltpu.SemaphoreType.DMA
    row = (1, PIECES)
    return pl.pallas_call(
        exchange_kernel,
        out_shape=(pltpu.VMEM((STRIP, PW), F32), pltpu.VMEM((STRIP, PW), F32)),
        in_specs=[pl.BlockSpec(memory_space=pl.ANY)] * 9,
        out_specs=(VMEM, VMEM),
        scratch_shapes=[
            pltpu.VMEM((8, PW), F32),
            pltpu.VMEM((PH + 2 * HALO, PW), F32),
            pltpu.VMEM((PW, PW), BF16),
            pltpu.VMEM((STRIP, PW), BF16),
            pltpu.VMEM(det_taps.shape, BF16),
            pltpu.SMEM((PIECES,), I32),
            pltpu.SMEM(coef_table.shape[::-1], F32),
            pltpu.VMEM(row, I32),
            pltpu.VMEM(row, I32),
            pltpu.VMEM(row, BF16),
            pltpu.VMEM(basis_col.shape, BF16),
            pltpu.VMEM(basis_row.shape, BF16),
            pltpu.VMEM((PIECES, PR, PW), BF16),
            pltpu.VMEM((NB * PW, PW), BF16),
            pltpu.VMEM((NB, 4, 8, PW), F32),
            pltpu.VMEM((GROUP * PR, NB * PW), BF16),
            pltpu.VMEM((32, PW), F32),
            pltpu.VMEM((8, PW), F32),
            pltpu.VMEM((8, PW), I32),
            pltpu.SMEM((8, PW), I32),
            pltpu.VMEM((PIECES + 8, PR, PW), BF16),
            pltpu.VMEM((16, ROWS, PW), BF16),
            pltpu.VMEM((16, ROWS, PW), BF16),
            pltpu.VMEM((16, META, PW), F32),
            pltpu.VMEM((VISITS, SIDE, LONG, PW), BF16),
            pltpu.VMEM((VISITS, SIDE, LONG, PW), BF16),
            pltpu.VMEM((SIDE, LONG, PW), BF16),
            pltpu.VMEM((SIDE, LONG, PW), BF16),
            dma((8,)),
            dma(()),
            dma(()),
            dma((CHUNKS, 16)),
            dma((CHUNKS, 16)),
            dma((CHUNKS, VISITS)),
            dma((CHUNKS, VISITS)),
            dma((SIDE,)),
            dma((SIDE,)),
        ],
        compiler_params=pltpu.CompilerParams(collective_id=0, has_side_effects=True),
        name="exchange",
    )(
        kernel_index, coef_table.T, dest.reshape(row), offsets.reshape(row), weights.reshape(row),
        basis_col, basis_row, det_taps, pieces,
    )


def shards(
    pieces, dest, offsets, kernel_index, weights, basis_col, basis_row, coef_table, det_taps
):
    return exchange(
        pieces, dest, offsets, kernel_index, weights, basis_col, basis_row, coef_table, det_taps
    )


def solution(mesh):
    split = P(("patch", "visit"))
    in_specs = (
        P(("patch", "visit"), None, None),
        P(("patch", "visit"), None),
        split,
        split,
        split,
        P(),
        P(),
        P(),
        P(),
    )
    out_specs = (P(("patch", "visit"), None), P(("patch", "visit"), None))
    return jax.shard_map(shards, mesh=mesh, in_specs=in_specs, out_specs=out_specs, check_vma=False)
```
